32 devices in a mesh: grp: 2 (over y), seq: 4 (over z), ch: 4 (over x, core).
Axes of the slice: x: 2, y: 2, z: 4, core: 2. Of those that a mesh axis runs over, the one named last changes fastest.
Arguments:
- activations: bfloat16 [4096, 1024], P('ch', ('grp', 'seq')), parts along dimension 1, may hold values from -6 to 6
- projection: bfloat16 [4096, 2048], P('seq', 'ch'), may hold values from -0.09375 to 0.09375
- medium_taps: float32 [2048, 128], P('ch'), may hold values from -0.5 to 0.5
- long_filters: bfloat16 [2048, 512], P('ch', 'seq'), may hold values from -0.25 to 0.25
- cotangent: bfloat16 [2048, 1024], P('ch', ('grp', 'seq')), parts along dimension 1, may hold values from -6 to 6
Outputs:
- conv_out: bfloat16 [2048, 1024], P('ch', ('grp', 'seq')), parts along dimension 1
- input_grad: bfloat16 [4096, 1024], P('ch', ('grp', 'seq')), parts along dimension 1
The draws below stay inside these ranges and needn't reach their ends.
There are 2 independent parts, one for each index of `grp`. The reference program is written for one: setup_inputs(seed, part) draws one part's arguments, and reference() takes and returns one part's arrays. A program takes and returns all parts, laid end to end along the dimension named above; an argument that names none is the same for every part. Nothing has to cross between parts.
All inputs are finite; a program needn't handle non-finite values.
Results may differ from the reference program's by a relative error of at most 0.012.
Values may be sent and summed in bfloat16 or wider, within the bound.
No kernel may reach another device: no remote copies, remote signals or barrier semaphores. Data moves between devices by JAX's collectives and lax.ppermute only.
A program may use at most 64 MiB of HBM per device.

```python
import jax
import jax.numpy as jnp
from jax import lax

D = 4096
C = 2048
K = 128
LENGTH = 512


def block_scale(rng, dims, split, smallest, top_value):
    factor_of, own = 1.0, jax.random.fold_in(rng, 6)
    for axis_at, shards_of in split:
        draws = jnp.exp(jax.random.uniform(jax.random.fold_in(own, axis_at), (shards_of,), jnp.float32, smallest / len(split), top_value / len(split)))
        factor_of = factor_of * jnp.repeat(draws, dims[axis_at] // shards_of).reshape([-1 if axis == axis_at else 1 for axis in range(len(dims))])
    return factor_of


def gaussian(own_key, extent, spread, bound, cuts=(), dtype=jnp.bfloat16):
    entries = spread * jax.random.normal(own_key, extent, jnp.float32)
    if cuts:
        entries = entries * block_scale(own_key, extent, cuts, -0.22, 0.18)
    return jnp.clip(entries, -bound, bound).astype(dtype)


def setup_inputs(seed: int = 0, part: int = 0) -> dict:
    splits = jax.random.split(jax.random.key(seed), 6)
    own_keys = jax.random.split(jax.random.fold_in(splits[5], part), 6)
    return {
        "activations": gaussian(own_keys[0], (D, LENGTH), 1.0, 6.0, ((0, 4), (1, 4))),
        "projection": gaussian(splits[1], (D, C), D ** -0.5, 0.09375, ((0, 4), (1, 4))),
        "medium_taps": gaussian(splits[2], (C, K), K ** -0.5, 0.5, ((0, 4),), jnp.float32),
        "long_filters": gaussian(splits[3], (C, LENGTH), LENGTH ** -0.5, 0.25, ((0, 4), (1, 4))),
        "cotangent": gaussian(own_keys[4], (C, LENGTH), 1.0, 6.0, ((0, 4), (1, 4))),
    }


def medium_forward(padded, tap_weights, length):
    tap_count = tap_weights.shape[1]
    summed = jnp.zeros((padded.shape[0], length), jnp.float32)
    for offset in range(tap_count):
        begin_col = tap_count - 1 - offset
        summed = summed + tap_weights[:, offset:offset + 1] * padded[:, begin_col:begin_col + length]
    return summed


def medium_backward(padded, tap_weights, length):
    tap_count = tap_weights.shape[1]
    summed = jnp.zeros((padded.shape[0], length), jnp.float32)
    for offset in range(tap_count):
        summed = summed + tap_weights[:, offset:offset + 1] * padded[:, offset:offset + length]
    return summed


def long_apply(signal, filter_row, conjugate):
    length = signal.shape[-1]
    points = 2 * length
    sig_spec = jnp.fft.rfft(signal, n=points, axis=-1)
    filt_spec = jnp.fft.rfft(filter_row, n=points, axis=-1)
    if conjugate:
        filt_spec = jnp.conj(filt_spec)
    return jnp.fft.irfft(sig_spec * filt_spec, n=points, axis=-1)[..., :length]


def long_blocks(signal, filters, conjugate):
    channels, length = signal.shape

    def run_block(operands):
        return long_apply(operands[0], operands[1], conjugate)

    result = lax.map(run_block, (signal.reshape(channels // 128, 128, length), filters.reshape(channels // 128, 128, length)))
    return result.reshape(channels, length)


def reference(activations, projection, medium_taps, long_filters, cotangent):
    tap_count = medium_taps.shape[1]
    length = activations.shape[1]
    values = jnp.dot(projection.T, activations, preferred_element_type=jnp.float32).astype(jnp.bfloat16)
    values_wide = values.astype(jnp.float32)
    gate_open = jax.nn.sigmoid(values_wide)
    medium = medium_forward(jnp.pad(values_wide, ((0, 0), (tap_count - 1, 0))), medium_taps, length)
    gated_conv = lax.optimization_barrier((medium * gate_open).astype(jnp.bfloat16))
    filters_wide = long_filters.astype(jnp.float32)
    conv_out = long_blocks(gated_conv.astype(jnp.float32), filters_wide, False).astype(jnp.bfloat16)
    grad_gated = lax.optimization_barrier(long_blocks(cotangent.astype(jnp.float32), filters_wide, True).astype(jnp.bfloat16))
    grad_wide = grad_gated.astype(jnp.float32)
    grad_medium = lax.optimization_barrier((grad_wide * gate_open).astype(jnp.bfloat16)).astype(jnp.float32)
    through = medium_backward(jnp.pad(grad_medium, ((0, 0), (0, tap_count - 1))), medium_taps, length)
    grad_values = (through + grad_wide * medium * gate_open * (1.0 - gate_open)).astype(jnp.bfloat16)
    input_grad = jnp.dot(projection, grad_values, preferred_element_type=jnp.float32).astype(jnp.bfloat16)
    return conv_out, input_grad
```

```python
import functools
import math

import jax
import jax.numpy as jnp
from jax import lax
from jax.experimental import pallas as pl
from jax.experimental.pallas import tpu as pltpu
from jax.sharding import PartitionSpec as P

exact_mode = lax.Precision.HIGH
F32 = jnp.float32
BF16 = jnp.bfloat16


def reverse_bits(value, count):
    out = 0
    for bit in range(count):
        out = out | (((value >> bit) & 1) << (count - 1 - bit))
    return out


def block_tables(size):
    steps = jnp.arange(size, dtype=jnp.int32)
    turns = (4 * steps[None, :] + 1) * steps[:, None] % (4 * size)
    angle = (2.0 * math.pi / (4 * size)) * turns.astype(F32)
    cos, sin = jnp.cos(angle), jnp.sin(angle)

    def parts(table):
        high = table.astype(BF16)
        return high, (table - high.astype(F32)).astype(BF16)

    forward = jnp.concatenate([cos, -sin], axis=1)
    inverse = jnp.concatenate([cos.T, -sin.T], axis=0) / size
    return (
        jnp.concatenate(parts(forward), axis=0),
        jnp.concatenate(parts(inverse), axis=1),
    )


def matmul(left, right):
    return jnp.dot(left, right, preferred_element_type=F32)


def to_spectrum(rows, table):
    size = rows.shape[1]
    out = matmul(jnp.concatenate([rows, rows], axis=1), table)
    return out[:, :size], out[:, size:]


def from_spectrum(real, imag, table):
    size = real.shape[1]
    both = jnp.concatenate([real, imag], axis=1)
    high = both.astype(BF16)
    low = (both - high.astype(F32)).astype(BF16)
    out = matmul(high, table)
    return out[:, :size] + out[:, size:] + matmul(low, table[:, :size])


def split_rows(array, count):
    step = array.shape[0] // count
    return [array[i * step : (i + 1) * step] for i in range(count)]


def prepare_kernel(n, index_ref, *refs):
    given, (taps_ref, table_ref, inverse_ref) = refs[:n], refs[n : n + 3]
    grad_ref, filt_ref, tap_ref, filters, cotangents = refs[n + 3 :]
    s = index_ref[0]
    size = taps_ref.shape[1]
    for r in range(n):
        filters[s ^ r] = given[r][0]
        cotangents[s ^ r] = given[r][1]
    table = table_ref[...]
    filt_re, filt_im = to_spectrum(filters[...].reshape(n * size, size), table)
    cot_re, cot_im = to_spectrum(cotangents[...].reshape(n * size, size), table)
    filt_ref[:, :size] = filt_re
    filt_ref[:, size:] = filt_im
    taps = taps_ref[pl.ds(pl.multiple_of(s * size, size), size), :]
    taps_high = taps.astype(BF16)
    taps_low = (taps - taps_high.astype(F32)).astype(BF16)
    tap_re, tap_im = to_spectrum(taps_high, table)
    rest = matmul(taps_low, table[:size])
    tap_ref[:, :size] = tap_re + rest[:, :size]
    tap_ref[:, size:] = tap_im + rest[:, size:]
    fr, fi = split_rows(filt_re, n), split_rows(filt_im, n)
    cr, ci = split_rows(cot_re, n), split_rows(cot_im, n)
    turned = []
    for b in range(n):
        if b + 1 < n:
            turned.append((cr[b] + ci[b + 1], ci[b] - cr[b + 1]))
        else:
            turned.append((cr[b], ci[b]))
    real, imag = [], []
    for b in range(n):
        re, im = 0.0, 0.0
        for d in range(n - b):
            vr, vi = turned[b + d]
            re = re + fr[d] * vr + fi[d] * vi
            im = im + fr[d] * vi - fi[d] * vr
        real.append(re)
        imag.append(im)
    out = from_spectrum(jnp.concatenate(real), jnp.concatenate(imag), inverse_ref[...])
    grad_ref[...] = out.astype(BF16).reshape(n, size, size)


def gate_kernel(n, index_ref, *refs):
    sums = refs[: 2 * n]
    grad_in_ref, tap_ref, table_ref, inverse_ref = refs[2 * n : 2 * n + 4]
    far_ref, near_ref, gated_ref, held = refs[2 * n + 4 :]
    c = index_ref[1]
    half, size = n // 2, tap_ref.shape[0]
    bits = n.bit_length() - 1
    for part in range(2):
        total = sums[part * n][...].astype(F32)
        for r in range(1, n):
            total = total + sums[part * n + r][...].astype(F32)
        for j in range(half):
            held[c ^ (part * half + j)] = total[j].astype(BF16)
    values = held[...].reshape(n * size, size)
    table, inverse = table_ref[...], inverse_ref[...]
    tr, ti = tap_ref[:, :size], tap_ref[:, size:]
    wide = values.astype(F32)
    gate = 1.0 / (1.0 + jnp.exp(-wide))
    grad = grad_in_ref[...].reshape(n * size, size).astype(F32)
    grad_medium = (grad * gate).astype(BF16)
    re, im = to_spectrum(values, table)
    gr, gi = to_spectrum(grad_medium, table)
    re, im, gr, gi = (split_rows(x, n) for x in (re, im, gr, gi))
    real, imag, back_real, back_imag = [], [], [], []
    for b in range(n):
        ur, ui = (re[b] - im[b - 1], im[b] + re[b - 1]) if b else (re[b], im[b])
        real.append(tr * ur - ti * ui)
        imag.append(tr * ui + ti * ur)
        vr, vi = (gr[b] + gi[b + 1], gi[b] - gr[b + 1]) if b + 1 < n else (gr[b], gi[b])
        back_real.append(tr * vr + ti * vi)
        back_imag.append(tr * vi - ti * vr)
    medium = from_spectrum(jnp.concatenate(real), jnp.concatenate(imag), inverse)
    through = from_spectrum(jnp.concatenate(back_real), jnp.concatenate(back_imag), inverse)
    gated_ref[...] = (medium * gate).astype(BF16).reshape(n, size, size)
    back = (through + grad * medium * gate * (1.0 - gate)).astype(BF16)
    held[...] = back.reshape(n, size, size)
    for j in range(half):
        near_ref[j] = held[reverse_bits(c ^ j, bits)]
        far_ref[j] = held[reverse_bits(c ^ (half + j), bits)]


def long_kernel(n, index_ref, gated_ref, filt_ref, table_ref, inverse_ref, *refs):
    outs, held = refs[:n], refs[n]
    s = index_ref[0]
    size = gated_ref.shape[2]
    re, im = to_spectrum(gated_ref[...].reshape(n * size, size), table_ref[...])
    re, im = split_rows(re, n), split_rows(im, n)
    fr, fi = split_rows(filt_ref[:, :size], n), split_rows(filt_ref[:, size:], n)
    turned = [(re[0], im[0])]
    for b in range(1, n):
        turned.append((re[b] - im[b - 1], im[b] + re[b - 1]))
    real, imag = [], []
    for b in range(n):
        zr, zi = 0.0, 0.0
        for d in range(b + 1):
            ur, ui = turned[b - d]
            zr = zr + fr[d] * ur - fi[d] * ui
            zi = zi + fr[d] * ui + fi[d] * ur
        real.append(zr)
        imag.append(zi)
    out = from_spectrum(jnp.concatenate(real), jnp.concatenate(imag), inverse_ref[...])
    held[...] = out.astype(BF16).reshape(n, size, size)
    for r in range(n):
        outs[r][...] = held[s ^ r]


def place_kernel(n, index_ref, *refs):
    given, out_ref = refs[:n], refs[n]
    s = index_ref[0]
    size = given[0].shape[0]
    for r in range(n):
        out_ref[pl.ds(pl.multiple_of((s ^ r) * size, size), size), :] = given[r][...]


def values_kernel(n, weight_ref, *refs):
    acts, outs = refs[: n // 2], refs[n // 2 :]
    size = acts[0].shape[1]
    right = jnp.concatenate([ref[...] for ref in acts], axis=1)
    step = weight_ref.shape[0] // n
    for r in range(n):
        out = matmul(weight_ref[r * step : (r + 1) * step, :], right).astype(BF16)
        for j in range(n // 2):
            outs[r][j] = out[:, j * size : (j + 1) * size]


def input_kernel(n, weight_ref, *refs):
    grads, outs = refs[:n], refs[n:]
    half = n // 2
    size = grads[0].shape[2]
    right = jnp.concatenate(
        [jnp.concatenate([ref[j] for j in range(half)], axis=1) for ref in grads], axis=0
    )
    out = matmul(weight_ref[...], right)
    for j in range(half):
        outs[j][...] = out[:, j * size : (j + 1) * size].astype(outs[j].dtype)


def call(kernel, outs, scratch, index, args, flops):
    sizes = sum(math.prod(a.shape) * a.dtype.itemsize for a in (*args, *outs))
    specs = [pl.BlockSpec(memory_space=pltpu.VMEM)] * len(args)
    if index is not None:
        specs = [pl.BlockSpec(memory_space=pltpu.SMEM)] + specs
        args = (index, *args)
    return pl.pallas_call(
        kernel,
        out_shape=tuple(outs),
        in_specs=specs,
        out_specs=tuple(pl.BlockSpec(memory_space=pltpu.VMEM) for _ in outs),
        scratch_shapes=scratch,
        cost_estimate=pl.CostEstimate(flops=flops, bytes_accessed=sizes, transcendentals=0),
    )(*args)


def square_plan(n, activations, projection, medium_taps, long_filters, cotangent):
    bits = n.bit_length() - 1
    half = n // 2
    depth, size = activations.shape
    own = projection.shape[1] // n
    s, c = lax.axis_index("seq"), lax.axis_index("ch")
    index = jnp.stack([s, c]).astype(jnp.int32)
    shape = jax.ShapeDtypeStruct

    def move(array, target):
        pairs = [
            (i * n + j, (lambda t: t[0] * n + t[1])(target(i, j)))
            for i in range(n)
            for j in range(n)
        ]
        return lax.ppermute(array, ("seq", "ch"), pairs)

    def across_seq(array, r):
        return move(array, lambda i, j: (i ^ r, j))

    def across_ch(array, r):
        return move(array, lambda i, j: (i, j ^ r))

    def gather_low(block):
        held = [block]
        while len(held) < half:
            step = len(held)
            held = held + [across_ch(x, step) for x in held]
        return held

    own_act = move(activations, lambda i, j: (j, i))

    both = jnp.stack([long_filters, cotangent]).reshape(2, n, own, size)
    blocks = [lax.dynamic_index_in_dim(both, s ^ r, 1, False) for r in range(n)]
    blocks = [blocks[0]] + [across_seq(blocks[r], r) for r in range(1, n)]

    columns = [
        lax.dynamic_slice_in_dim(projection, (s ^ r) * own, own, 1) for r in range(n)
    ]
    weight = jnp.concatenate(columns, axis=1)
    weight, weight_t = lax.optimization_barrier((weight, weight.T))
    table, inverse = lax.optimization_barrier(block_tables(size))

    def values_of(acts):
        outs = [shape((half, own, size), BF16)] * n
        parts = call(
            functools.partial(values_kernel, n),
            outs,
            [],
            None,
            (weight_t, *acts),
            2 * depth * n * own * half * size,
        )
        return [parts[0]] + [across_seq(parts[r], r) for r in range(1, n)]

    far_act = across_ch(own_act, half)
    near_sums = values_of(gather_low(own_act))
    far_sums = values_of(gather_low(far_act))

    spectrum = 4 * n * size * 2 * size * own
    grad_gated, filt, tap = call(
        functools.partial(prepare_kernel, n),
        [shape((n, own, size), BF16), shape((n * own, 2 * size), F32), shape((own, 2 * size), F32)],
        [pltpu.VMEM((n, own, size), BF16), pltpu.VMEM((n, own, size), BF16)],
        index,
        (*blocks, medium_taps, table, inverse),
        6 * spectrum,
    )
    far, near, gated = call(
        functools.partial(gate_kernel, n),
        [shape((half, own, size), BF16), shape((half, own, size), BF16), shape((n, own, size), BF16)],
        [pltpu.VMEM((n, own, size), BF16)],
        index,
        (*near_sums, *far_sums, grad_gated, tap, table, inverse),
        8 * spectrum,
    )

    def gathered(part):
        return [part] + [across_seq(part, r) for r in range(1, n)]

    far_parts = gathered(far)
    near_parts = gathered(near)

    out_blocks = call(
        functools.partial(long_kernel, n),
        [shape((own, size), BF16)] * n,
        [pltpu.VMEM((n, own, size), BF16)],
        index,
        (gated, filt, table, inverse),
        4 * spectrum,
    )
    out_blocks = [out_blocks[0]] + [across_seq(out_blocks[r], r) for r in range(1, n)]

    def input_of(parts):
        outs = [shape((depth, size), F32 if j < max(half // 2, 1) else BF16) for j in range(half)]
        return call(
            functools.partial(input_kernel, n),
            outs,
            [],
            None,
            (weight, *parts),
            2 * depth * n * own * half * size,
        )

    def scatter_low(sums):
        while len(sums) > 1:
            step = len(sums) // 2
            kept = sums[:step]
            sent = [across_ch(x.astype(BF16), step) for x in sums[step:]]
            sums = [a.astype(F32) + b.astype(F32) for a, b in zip(kept, sent)]
        return sums[0]

    far_total = across_ch(scatter_low(list(input_of(far_parts))).astype(BF16), half)
    total = scatter_low(list(input_of(near_parts))) + far_total.astype(F32)
    input_grad = move(total.astype(BF16), lambda i, j: (reverse_bits(j, bits), i))
    (conv_out,) = call(
        functools.partial(place_kernel, n),
        [shape((n * own, size), BF16)],
        [],
        index,
        tuple(out_blocks),
        0,
    )
    return conv_out, input_grad


def medium_forward(padded, tap_weights, length):
    tap_count = tap_weights.shape[1]
    summed = jnp.zeros((padded.shape[0], length), jnp.float32)
    for offset in range(tap_count):
        begin_col = tap_count - 1 - offset
        summed = (
            summed + tap_weights[:, offset : offset + 1] * padded[:, begin_col : begin_col + length]
        )
    return summed


def medium_backward(padded, tap_weights, length):
    tap_count = tap_weights.shape[1]
    summed = jnp.zeros((padded.shape[0], length), jnp.float32)
    for offset in range(tap_count):
        summed = summed + tap_weights[:, offset : offset + 1] * padded[:, offset : offset + length]
    return summed


def dft_tables(length):
    points = 2 * length
    columns = 128
    row_count = points // columns
    half_rows = row_count // 2
    freq_rows = jnp.arange(row_count, dtype=jnp.int32)
    time_rows = jnp.arange(half_rows, dtype=jnp.int32)
    lane_index = jnp.arange(columns, dtype=jnp.int32)
    angle_first = (
        2.0
        * math.pi
        / row_count
        * (freq_rows[:, None] * time_rows[None, :] % row_count).astype(jnp.float32)
    )
    angle_twist = (
        2.0
        * math.pi
        / points
        * (freq_rows[:, None] * lane_index[None, :] % points).astype(jnp.float32)
    )
    angle_last = (
        2.0
        * math.pi
        / columns
        * (lane_index[:, None] * lane_index[None, :] % columns).astype(jnp.float32)
    )
    return (
        jnp.cos(angle_first),
        jnp.sin(angle_first),
        jnp.cos(angle_twist),
        jnp.sin(angle_twist),
        jnp.cos(angle_last),
        jnp.sin(angle_last),
    )


def forward_dft(signal, tables):
    cos_first, sin_first, cos_twist, sin_twist, cos_last, sin_last = tables
    channels = signal.shape[0]
    shaped = signal.reshape(channels, cos_first.shape[1], 128)
    section_re = jnp.einsum("kn,cnq->ckq", cos_first, shaped, precision=exact_mode)
    section_im = -jnp.einsum("kn,cnq->ckq", sin_first, shaped, precision=exact_mode)
    twist_re = section_re * cos_twist + section_im * sin_twist
    twist_im = section_im * cos_twist - section_re * sin_twist
    spec_re = jnp.einsum("ckq,qm->ckm", twist_re, cos_last, precision=exact_mode) + jnp.einsum(
        "ckq,qm->ckm", twist_im, sin_last, precision=exact_mode
    )
    spec_im = jnp.einsum("ckq,qm->ckm", twist_im, cos_last, precision=exact_mode) - jnp.einsum(
        "ckq,qm->ckm", twist_re, sin_last, precision=exact_mode
    )
    return (spec_re, spec_im)


def inverse_dft(spec_re, spec_im, tables):
    cos_first, sin_first, cos_twist, sin_twist, cos_last, sin_last = tables
    channels = spec_re.shape[0]
    half_rows = cos_first.shape[1]
    inner_re = jnp.einsum("ckq,qm->ckm", spec_re, cos_last, precision=exact_mode) - jnp.einsum(
        "ckq,qm->ckm", spec_im, sin_last, precision=exact_mode
    )
    inner_im = jnp.einsum("ckq,qm->ckm", spec_im, cos_last, precision=exact_mode) + jnp.einsum(
        "ckq,qm->ckm", spec_re, sin_last, precision=exact_mode
    )
    turned_re = inner_re * cos_twist - inner_im * sin_twist
    turned_im = inner_im * cos_twist + inner_re * sin_twist
    output = jnp.einsum("kn,ckq->cnq", cos_first, turned_re, precision=exact_mode) - jnp.einsum(
        "kn,ckq->cnq", sin_first, turned_im, precision=exact_mode
    )
    points = 2 * half_rows * 128
    return (output / points).reshape(channels, half_rows * 128)


def causal_apply(signal, filt_re, filt_im, tables, conjugate):
    sig_re, sig_im = forward_dft(signal, tables)
    if conjugate:
        prod_re = sig_re * filt_re + sig_im * filt_im
        prod_im = sig_im * filt_re - sig_re * filt_im
    else:
        prod_re = sig_re * filt_re - sig_im * filt_im
        prod_im = sig_im * filt_re + sig_re * filt_im
    return inverse_dft(prod_re, prod_im, tables)


def on_device(activations, projection, medium_taps, long_filters, cotangent):
    tap_count = medium_taps.shape[1]
    whole_in = lax.all_gather(activations, "ch", axis=0, tiled=True)
    mixed_sum = lax.dot_general(
        lax.all_gather(projection, "seq", axis=0, tiled=True),
        whole_in,
        (((0,), (0,)), ((), ())),
        preferred_element_type=jnp.float32,
    )
    values = mixed_sum.astype(jnp.bfloat16)
    channel_count = values.shape[0] // lax.axis_size("seq")
    own_taps = lax.dynamic_slice_in_dim(
        medium_taps, lax.axis_index("seq") * channel_count, channel_count, 0
    )
    arrived, filters_ch = (
        lax.all_to_all(values, "seq", split_axis=0, concat_axis=1, tiled=True),
        lax.all_to_all(long_filters, "seq", split_axis=0, concat_axis=1, tiled=True),
    )
    tables = dft_tables(arrived.shape[1])
    filt_re, filt_im = forward_dft(filters_ch.astype(jnp.float32), tables)
    values_ch = arrived.astype(jnp.float32)
    padded_ch = jnp.pad(values_ch, ((0, 0), (tap_count - 1, 0)))
    conv_ch = medium_forward(padded_ch, own_taps, arrived.shape[1])
    gate_ch = jax.nn.sigmoid(values_ch)
    signal = lax.optimization_barrier((conv_ch * gate_ch).astype(jnp.bfloat16)).astype(jnp.float32)
    kept_state = (conv_ch, gate_ch)
    output_ch = causal_apply(signal, filt_re, filt_im, tables, False).astype(jnp.bfloat16)
    output_ch, context = (output_ch, (filt_re, filt_im, tables, kept_state))
    conv_out = lax.all_to_all(output_ch, "seq", split_axis=1, concat_axis=0, tiled=True)
    grad_ch = lax.all_to_all(cotangent, "seq", split_axis=0, concat_axis=1, tiled=True)
    filt_re, filt_im, tables, kept_state = context
    back_grad = lax.optimization_barrier(
        causal_apply(grad_ch.astype(jnp.float32), filt_re, filt_im, tables, True).astype(
            jnp.bfloat16
        )
    )
    conv_ch, gate_ch = kept_state
    grad_wide = back_grad.astype(jnp.float32)
    conv_grad = lax.optimization_barrier((grad_wide * gate_ch).astype(jnp.bfloat16)).astype(
        jnp.float32
    )
    padded_grad = jnp.pad(conv_grad, ((0, 0), (0, tap_count - 1)))
    through = medium_backward(padded_grad, own_taps, conv_grad.shape[1])
    gate_grad = grad_wide * conv_ch * gate_ch * (1.0 - gate_ch)
    back_ch = (through + gate_grad).astype(jnp.bfloat16)
    returned = lax.all_to_all(back_ch, "seq", split_axis=1, concat_axis=0, tiled=True)
    partial_grad = jnp.dot(
        lax.all_gather(projection, "seq", axis=0, tiled=True),
        returned,
        preferred_element_type=jnp.float32,
    )
    input_grad = lax.psum_scatter(
        partial_grad.astype(jnp.bfloat16), "ch", scatter_dimension=0, tiled=True
    )
    return (conv_out, input_grad)


def solution(mesh):
    seq, ch = mesh.shape["seq"], mesh.shape["ch"]

    def step(*args):
        activations, projection, medium_taps = args[:3]
        size = activations.shape[1]
        square = (
            seq == ch
            and seq > 1
            and seq & (seq - 1) == 0
            and medium_taps.shape[1] == size
            and projection.shape[0] == activations.shape[0]
            and projection.shape[1] == seq * size
            and size % 128 == 0
        )
        return square_plan(seq, *args) if square else on_device(*args)

    return jax.shard_map(
        step,
        mesh=mesh,
        in_specs=(
            P("ch", ("grp", "seq")),
            P("seq", "ch"),
            P("ch", None),
            P("ch", "seq"),
            P("ch", ("grp", "seq")),
        ),
        out_specs=(P("ch", ("grp", "seq")), P("ch", ("grp", "seq"))),
        check_vma=False,
    )
```

```python
import functools
import math

import jax
import jax.numpy as jnp
from jax import lax
from jax.experimental import pallas as pl
from jax.experimental.pallas import tpu as pltpu
from jax.sharding import PartitionSpec as P


exact_mode = lax.Precision.HIGH
F32 = jnp.float32
BF16 = jnp.bfloat16


def reverse_bits(value, count):
    out = 0
    for bit in range(count):
        out = out | (((value >> bit) & 1) << (count - 1 - bit))
    return out


def block_tables(size):
    steps = jnp.arange(size, dtype=jnp.int32)
    turns = (4 * steps[None, :] + 1) * steps[:, None] % (4 * size)
    angle = (2.0 * math.pi / (4 * size)) * turns.astype(F32)
    cos, sin = jnp.cos(angle), jnp.sin(angle)

    def parts(table):
        high = table.astype(BF16)
        return high, (table - high.astype(F32)).astype(BF16)

    forward = jnp.concatenate([cos, -sin], axis=1)
    inverse = jnp.concatenate([cos.T, -sin.T], axis=0) / size
    return (
        jnp.concatenate(parts(forward), axis=0),
        jnp.concatenate(parts(inverse), axis=1),
    )


def matmul(left, right):
    return jnp.dot(left, right, preferred_element_type=F32)


def to_spectrum(rows, table):
    size = rows.shape[1]
    out = matmul(jnp.concatenate([rows, rows], axis=1), table)
    return out[:, :size], out[:, size:]


def from_spectrum(real, imag, table):
    size = real.shape[1]
    both = jnp.concatenate([real, imag], axis=1)
    high = both.astype(BF16)
    low = (both - high.astype(F32)).astype(BF16)
    out = matmul(high, table)
    return out[:, :size] + out[:, size:] + matmul(low, table[:, :size])


def split_rows(array, count):
    step = array.shape[0] // count
    return [array[i * step : (i + 1) * step] for i in range(count)]


def prepare_kernel(n, index_ref, *refs):
    given, (taps_ref, table_ref, inverse_ref) = refs[:n], refs[n : n + 3]
    grad_ref, filt_ref, tap_ref, filters, cotangents = refs[n + 3 :]
    s = index_ref[0]
    size = taps_ref.shape[1]
    for r in range(n):
        filters[s ^ r] = given[r][0]
        cotangents[s ^ r] = given[r][1]
    table = table_ref[...]
    filt_re, filt_im = to_spectrum(filters[...].reshape(n * size, size), table)
    cot_re, cot_im = to_spectrum(cotangents[...].reshape(n * size, size), table)
    filt_ref[:, :size] = filt_re
    filt_ref[:, size:] = filt_im
    taps = taps_ref[pl.ds(pl.multiple_of(s * size, size), size), :]
    taps_high = taps.astype(BF16)
    taps_low = (taps - taps_high.astype(F32)).astype(BF16)
    tap_re, tap_im = to_spectrum(taps_high, table)
    rest = matmul(taps_low, table[:size])
    tap_ref[:, :size] = tap_re + rest[:, :size]
    tap_ref[:, size:] = tap_im + rest[:, size:]
    fr, fi = split_rows(filt_re, n), split_rows(filt_im, n)
    cr, ci = split_rows(cot_re, n), split_rows(cot_im, n)
    turned = []
    for b in range(n):
        if b + 1 < n:
            turned.append((cr[b] + ci[b + 1], ci[b] - cr[b + 1]))
        else:
            turned.append((cr[b], ci[b]))
    real, imag = [], []
    for b in range(n):
        re, im = 0.0, 0.0
        for d in range(n - b):
            vr, vi = turned[b + d]
            re = re + fr[d] * vr + fi[d] * vi
            im = im + fr[d] * vi - fi[d] * vr
        real.append(re)
        imag.append(im)
    out = from_spectrum(jnp.concatenate(real), jnp.concatenate(imag), inverse_ref[...])
    grad_ref[...] = out.astype(BF16).reshape(n, size, size)


def gate_kernel(n, index_ref, *refs):
    sums = refs[: 2 * n]
    grad_in_ref, tap_ref, table_ref, inverse_ref = refs[2 * n : 2 * n + 4]
    far_ref, near_ref, gated_ref, held = refs[2 * n + 4 :]
    c = index_ref[1]
    half, size = n // 2, tap_ref.shape[0]
    bits = n.bit_length() - 1
    for part in range(2):
        total = sums[part * n][...].astype(F32)
        for r in range(1, n):
            total = total + sums[part * n + r][...].astype(F32)
        for j in range(half):
            held[c ^ (part * half + j)] = total[j].astype(BF16)
    values = held[...].reshape(n * size, size)
    table, inverse = table_ref[...], inverse_ref[...]
    tr, ti = tap_ref[:, :size], tap_ref[:, size:]
    wide = values.astype(F32)
    gate = 1.0 / (1.0 + jnp.exp(-wide))
    grad = grad_in_ref[...].reshape(n * size, size).astype(F32)
    grad_medium = (grad * gate).astype(BF16)
    re, im = to_spectrum(values, table)
    gr, gi = to_spectrum(grad_medium, table)
    re, im, gr, gi = (split_rows(x, n) for x in (re, im, gr, gi))
    real, imag, back_real, back_imag = [], [], [], []
    for b in range(n):
        ur, ui = (re[b] - im[b - 1], im[b] + re[b - 1]) if b else (re[b], im[b])
        real.append(tr * ur - ti * ui)
        imag.append(tr * ui + ti * ur)
        vr, vi = (gr[b] + gi[b + 1], gi[b] - gr[b + 1]) if b + 1 < n else (gr[b], gi[b])
        back_real.append(tr * vr + ti * vi)
        back_imag.append(tr * vi - ti * vr)
    medium = from_spectrum(jnp.concatenate(real), jnp.concatenate(imag), inverse)
    through = from_spectrum(jnp.concatenate(back_real), jnp.concatenate(back_imag), inverse)
    gated_ref[...] = (medium * gate).astype(BF16).reshape(n, size, size)
    back = (through + grad * medium * gate * (1.0 - gate)).astype(BF16)
    held[...] = back.reshape(n, size, size)
    for j in range(half):
        near_ref[j] = held[reverse_bits(c ^ j, bits)]
        far_ref[j] = held[reverse_bits(c ^ (half + j), bits)]


def long_kernel(n, index_ref, gated_ref, filt_ref, table_ref, inverse_ref, *refs):
    outs, held = refs[:n], refs[n]
    s = index_ref[0]
    size = gated_ref.shape[2]
    re, im = to_spectrum(gated_ref[...].reshape(n * size, size), table_ref[...])
    re, im = split_rows(re, n), split_rows(im, n)
    fr, fi = split_rows(filt_ref[:, :size], n), split_rows(filt_ref[:, size:], n)
    turned = [(re[0], im[0])]
    for b in range(1, n):
        turned.append((re[b] - im[b - 1], im[b] + re[b - 1]))
    real, imag = [], []
    for b in range(n):
        zr, zi = 0.0, 0.0
        for d in range(b + 1):
            ur, ui = turned[b - d]
            zr = zr + fr[d] * ur - fi[d] * ui
            zi = zi + fr[d] * ui + fi[d] * ur
        real.append(zr)
        imag.append(zi)
    out = from_spectrum(jnp.concatenate(real), jnp.concatenate(imag), inverse_ref[...])
    held[...] = out.astype(BF16).reshape(n, size, size)
    for r in range(n):
        outs[r][...] = held[s ^ r]


def place_kernel(n, index_ref, *refs):
    given, out_ref = refs[:n], refs[n]
    s = index_ref[0]
    size = given[0].shape[0]
    for r in range(n):
        out_ref[pl.ds(pl.multiple_of((s ^ r) * size, size), size), :] = given[r][...]


def arrange_kernel(n, index_ref, given_ref, filters_ref, cotangent_ref, *refs):
    weight_ref, turned_ref, blocks = refs[0], refs[1], refs[2:]
    s = index_ref[0]
    size = given_ref.shape[1] // n
    for r in range(n):
        start = pl.multiple_of((s ^ r) * size, size)
        blocks[r][0] = filters_ref[pl.ds(start, size), :]
        blocks[r][1] = cotangent_ref[pl.ds(start, size), :]
        block = given_ref[:, pl.ds(start, size)]
        weight_ref[:, r * size : (r + 1) * size] = block
        turned_ref[r * size : (r + 1) * size, :] = block.T


def values_kernel(n, weight_ref, *refs):
    acts, outs = refs[: n // 2], refs[n // 2 :]
    size = acts[0].shape[1]
    right = jnp.concatenate([ref[...] for ref in acts], axis=1)
    step = weight_ref.shape[0] // n
    for r in range(n):
        out = matmul(weight_ref[r * step : (r + 1) * step, :], right).astype(BF16)
        for j in range(n // 2):
            outs[r][j] = out[:, j * size : (j + 1) * size]


def input_kernel(n, weight_ref, *refs):
    grads, outs = refs[:n], refs[n:]
    half = n // 2
    size = grads[0].shape[2]
    right = jnp.concatenate(
        [jnp.concatenate([ref[j] for j in range(half)], axis=1) for ref in grads], axis=0
    )
    out = matmul(weight_ref[...], right)
    for j in range(half):
        outs[j][...] = out[:, j * size : (j + 1) * size].astype(outs[j].dtype)


def call(kernel, outs, scratch, index, args, flops):
    sizes = sum(math.prod(a.shape) * a.dtype.itemsize for a in (*args, *outs))
    held = sum(math.prod(a.shape) * jnp.dtype(a.dtype).itemsize for a in scratch)
    specs = [pl.BlockSpec(memory_space=pltpu.VMEM)] * len(args)
    if index is not None:
        specs = [pl.BlockSpec(memory_space=pltpu.SMEM)] + specs
        args = (index, *args)
    return pl.pallas_call(
        kernel,
        out_shape=tuple(outs),
        in_specs=specs,
        out_specs=tuple(pl.BlockSpec(memory_space=pltpu.VMEM) for _ in outs),
        scratch_shapes=scratch,
        cost_estimate=pl.CostEstimate(flops=flops, bytes_accessed=sizes, transcendentals=0),
        compiler_params=pltpu.CompilerParams(vmem_limit_bytes=3 * (sizes + held) + (4 << 20)),
    )(*args)


def square_plan(n, activations, projection, medium_taps, long_filters, cotangent):
    bits = n.bit_length() - 1
    half = n // 2
    depth, size = activations.shape
    own = projection.shape[1] // n
    s, c = lax.axis_index("seq"), lax.axis_index("ch")
    index = jnp.stack([s, c]).astype(jnp.int32)
    shape = jax.ShapeDtypeStruct

    def move(array, target):
        pairs = [
            (i * n + j, (lambda t: t[0] * n + t[1])(target(i, j)))
            for i in range(n)
            for j in range(n)
        ]
        return lax.ppermute(array, ("seq", "ch"), pairs)

    def across_seq(array, r):
        return move(array, lambda i, j: (i ^ r, j))

    def across_ch(array, r):
        return move(array, lambda i, j: (i, j ^ r))

    def spread(parts):
        return [parts[0]] + [across_seq(parts[r], r) for r in range(1, n)]

    def gather_low(block):
        held = [block]
        while len(held) < half:
            step = len(held)
            held = held + [across_ch(x, step) for x in held]
        return held

    act = move(activations, lambda i, j: (j, i))
    weight, weight_t, *blocks = call(
        functools.partial(arrange_kernel, n),
        [shape(projection.shape, BF16), shape(projection.shape[::-1], BF16)]
        + [shape((2, own, size), BF16)] * n,
        [],
        index,
        (projection, long_filters, cotangent),
        0,
    )
    table, inverse = block_tables(size)
    act, weight, weight_t, table, inverse, *blocks = lax.optimization_barrier(
        (act, weight, weight_t, table, inverse, *blocks)
    )

    def values_of(acts):
        return call(
            functools.partial(values_kernel, n),
            [shape((half, own, size), BF16)] * n,
            [],
            None,
            (weight_t, *acts),
            2 * depth * n * own * half * size,
        )

    far_act = across_ch(act, half)
    blocks = spread(blocks)
    near_sums = spread(values_of(gather_low(act)))
    far_sums = spread(values_of(gather_low(far_act)))

    spectrum = 4 * n * size * 2 * size * own
    grad_gated, filt, tap = call(
        functools.partial(prepare_kernel, n),
        [shape((n, own, size), BF16), shape((n * own, 2 * size), F32), shape((own, 2 * size), F32)],
        [pltpu.VMEM((n, own, size), BF16), pltpu.VMEM((n, own, size), BF16)],
        index,
        (*blocks, medium_taps, table, inverse),
        6 * spectrum,
    )
    far, near, gated = call(
        functools.partial(gate_kernel, n),
        [shape((half, own, size), BF16), shape((half, own, size), BF16), shape((n, own, size), BF16)],
        [pltpu.VMEM((n, own, size), BF16)],
        index,
        (*near_sums, *far_sums, grad_gated, tap, table, inverse),
        8 * spectrum,
    )
    far_back = spread([far] * n)
    near_back = spread([near] * n)

    out_blocks = call(
        functools.partial(long_kernel, n),
        [shape((own, size), BF16)] * n,
        [pltpu.VMEM((n, own, size), BF16)],
        index,
        (gated, filt, table, inverse),
        4 * spectrum,
    )
    out_blocks = spread(out_blocks)

    def input_of(parts):
        outs = [shape((depth, size), F32 if j < max(half // 2, 1) else BF16) for j in range(half)]
        return call(
            functools.partial(input_kernel, n),
            outs,
            [],
            None,
            (weight, *parts),
            2 * depth * n * own * half * size,
        )

    def scatter_low(sums):
        while len(sums) > 1:
            step = len(sums) // 2
            kept = sums[:step]
            sent = [across_ch(x.astype(BF16), step) for x in sums[step:]]
            sums = [a.astype(F32) + b.astype(F32) for a, b in zip(kept, sent)]
        return sums[0]

    far_total = scatter_low(list(input_of(far_back))).astype(BF16)
    far_total = across_ch(far_total, half)
    total = scatter_low(list(input_of(near_back)))
    total = total + far_total.astype(F32)
    input_grad = move(total.astype(BF16), lambda i, j: (reverse_bits(j, bits), i))
    (conv_out,) = call(
        functools.partial(place_kernel, n),
        [shape((n * own, size), BF16)],
        [],
        index,
        tuple(out_blocks),
        0,
    )
    return conv_out, input_grad


def medium_forward(padded, tap_weights, length):
    tap_count = tap_weights.shape[1]
    summed = jnp.zeros((padded.shape[0], length), jnp.float32)
    for offset in range(tap_count):
        begin_col = tap_count - 1 - offset
        summed = (
            summed + tap_weights[:, offset : offset + 1] * padded[:, begin_col : begin_col + length]
        )
    return summed


def medium_backward(padded, tap_weights, length):
    tap_count = tap_weights.shape[1]
    summed = jnp.zeros((padded.shape[0], length), jnp.float32)
    for offset in range(tap_count):
        summed = summed + tap_weights[:, offset : offset + 1] * padded[:, offset : offset + length]
    return summed


def dft_tables(length):
    points = 2 * length
    columns = 128
    row_count = points // columns
    half_rows = row_count // 2
    freq_rows = jnp.arange(row_count, dtype=jnp.int32)
    time_rows = jnp.arange(half_rows, dtype=jnp.int32)
    lane_index = jnp.arange(columns, dtype=jnp.int32)
    angle_first = (
        2.0
        * math.pi
        / row_count
        * (freq_rows[:, None] * time_rows[None, :] % row_count).astype(jnp.float32)
    )
    angle_twist = (
        2.0
        * math.pi
        / points
        * (freq_rows[:, None] * lane_index[None, :] % points).astype(jnp.float32)
    )
    angle_last = (
        2.0
        * math.pi
        / columns
        * (lane_index[:, None] * lane_index[None, :] % columns).astype(jnp.float32)
    )
    return (
        jnp.cos(angle_first),
        jnp.sin(angle_first),
        jnp.cos(angle_twist),
        jnp.sin(angle_twist),
        jnp.cos(angle_last),
        jnp.sin(angle_last),
    )


def forward_dft(signal, tables):
    cos_first, sin_first, cos_twist, sin_twist, cos_last, sin_last = tables
    channels = signal.shape[0]
    shaped = signal.reshape(channels, cos_first.shape[1], 128)
    section_re = jnp.einsum("kn,cnq->ckq", cos_first, shaped, precision=exact_mode)
    section_im = -jnp.einsum("kn,cnq->ckq", sin_first, shaped, precision=exact_mode)
    twist_re = section_re * cos_twist + section_im * sin_twist
    twist_im = section_im * cos_twist - section_re * sin_twist
    spec_re = jnp.einsum("ckq,qm->ckm", twist_re, cos_last, precision=exact_mode) + jnp.einsum(
        "ckq,qm->ckm", twist_im, sin_last, precision=exact_mode
    )
    spec_im = jnp.einsum("ckq,qm->ckm", twist_im, cos_last, precision=exact_mode) - jnp.einsum(
        "ckq,qm->ckm", twist_re, sin_last, precision=exact_mode
    )
    return (spec_re, spec_im)


def inverse_dft(spec_re, spec_im, tables):
    cos_first, sin_first, cos_twist, sin_twist, cos_last, sin_last = tables
    channels = spec_re.shape[0]
    half_rows = cos_first.shape[1]
    inner_re = jnp.einsum("ckq,qm->ckm", spec_re, cos_last, precision=exact_mode) - jnp.einsum(
        "ckq,qm->ckm", spec_im, sin_last, precision=exact_mode
    )
    inner_im = jnp.einsum("ckq,qm->ckm", spec_im, cos_last, precision=exact_mode) + jnp.einsum(
        "ckq,qm->ckm", spec_re, sin_last, precision=exact_mode
    )
    turned_re = inner_re * cos_twist - inner_im * sin_twist
    turned_im = inner_im * cos_twist + inner_re * sin_twist
    output = jnp.einsum("kn,ckq->cnq", cos_first, turned_re, precision=exact_mode) - jnp.einsum(
        "kn,ckq->cnq", sin_first, turned_im, precision=exact_mode
    )
    points = 2 * half_rows * 128
    return (output / points).reshape(channels, half_rows * 128)


def causal_apply(signal, filt_re, filt_im, tables, conjugate):
    sig_re, sig_im = forward_dft(signal, tables)
    if conjugate:
        prod_re = sig_re * filt_re + sig_im * filt_im
        prod_im = sig_im * filt_re - sig_re * filt_im
    else:
        prod_re = sig_re * filt_re - sig_im * filt_im
        prod_im = sig_im * filt_re + sig_re * filt_im
    return inverse_dft(prod_re, prod_im, tables)


def on_device(activations, projection, medium_taps, long_filters, cotangent):
    tap_count = medium_taps.shape[1]
    whole_in = lax.all_gather(activations, "ch", axis=0, tiled=True)
    mixed_sum = lax.dot_general(
        lax.all_gather(projection, "seq", axis=0, tiled=True),
        whole_in,
        (((0,), (0,)), ((), ())),
        preferred_element_type=jnp.float32,
    )
    values = mixed_sum.astype(jnp.bfloat16)
    channel_count = values.shape[0] // lax.axis_size("seq")
    own_taps = lax.dynamic_slice_in_dim(
        medium_taps, lax.axis_index("seq") * channel_count, channel_count, 0
    )
    arrived, filters_ch = (
        lax.all_to_all(values, "seq", split_axis=0, concat_axis=1, tiled=True),
        lax.all_to_all(long_filters, "seq", split_axis=0, concat_axis=1, tiled=True),
    )
    tables = dft_tables(arrived.shape[1])
    filt_re, filt_im = forward_dft(filters_ch.astype(jnp.float32), tables)
    values_ch = arrived.astype(jnp.float32)
    padded_ch = jnp.pad(values_ch, ((0, 0), (tap_count - 1, 0)))
    conv_ch = medium_forward(padded_ch, own_taps, arrived.shape[1])
    gate_ch = jax.nn.sigmoid(values_ch)
    signal = lax.optimization_barrier((conv_ch * gate_ch).astype(jnp.bfloat16)).astype(jnp.float32)
    kept_state = (conv_ch, gate_ch)
    output_ch = causal_apply(signal, filt_re, filt_im, tables, False).astype(jnp.bfloat16)
    output_ch, context = (output_ch, (filt_re, filt_im, tables, kept_state))
    conv_out = lax.all_to_all(output_ch, "seq", split_axis=1, concat_axis=0, tiled=True)
    grad_ch = lax.all_to_all(cotangent, "seq", split_axis=0, concat_axis=1, tiled=True)
    filt_re, filt_im, tables, kept_state = context
    back_grad = lax.optimization_barrier(
        causal_apply(grad_ch.astype(jnp.float32), filt_re, filt_im, tables, True).astype(
            jnp.bfloat16
        )
    )
    conv_ch, gate_ch = kept_state
    grad_wide = back_grad.astype(jnp.float32)
    conv_grad = lax.optimization_barrier((grad_wide * gate_ch).astype(jnp.bfloat16)).astype(
        jnp.float32
    )
    padded_grad = jnp.pad(conv_grad, ((0, 0), (0, tap_count - 1)))
    through = medium_backward(padded_grad, own_taps, conv_grad.shape[1])
    gate_grad = grad_wide * conv_ch * gate_ch * (1.0 - gate_ch)
    back_ch = (through + gate_grad).astype(jnp.bfloat16)
    returned = lax.all_to_all(back_ch, "seq", split_axis=1, concat_axis=0, tiled=True)
    partial_grad = jnp.dot(
        lax.all_gather(projection, "seq", axis=0, tiled=True),
        returned,
        preferred_element_type=jnp.float32,
    )
    input_grad = lax.psum_scatter(
        partial_grad.astype(jnp.bfloat16), "ch", scatter_dimension=0, tiled=True
    )
    return (conv_out, input_grad)


def fits_square(mesh, activations, projection, medium_taps):
    seq, ch = mesh.shape["seq"], mesh.shape["ch"]
    size = activations.shape[1] // (mesh.shape["grp"] * seq)
    return (
        seq == ch
        and seq > 1
        and seq & (seq - 1) == 0
        and medium_taps.shape[1] == size
        and projection.shape[1] == seq * ch * size
        and size % 128 == 0
        and activations.shape[0] % (2 * ch * size) == 0
    )


def solution(mesh):
    n = mesh.shape["seq"]

    def placed(body):
        return jax.shard_map(
            body,
            mesh=mesh,
            in_specs=(
                P("ch", ("grp", "seq")),
                P("seq", "ch"),
                P("ch", None),
                P("ch", "seq"),
                P("ch", ("grp", "seq")),
            ),
            out_specs=(P("ch", ("grp", "seq")), P("ch", ("grp", "seq"))),
            check_vma=False,
        )

    def square(*args):
        return square_plan(n, *args)

    def step(*args):
        return placed(square if fits_square(mesh, *args[:3]) else on_device)(*args)

    if mesh.shape["seq"] != mesh.shape["ch"]:
        return step
    return step
```

```python
import functools
import math

import jax
import jax.numpy as jnp
from jax import lax
from jax.experimental import pallas as pl
from jax.experimental.pallas import tpu as pltpu
from jax.sharding import PartitionSpec as P


exact_mode = lax.Precision.HIGH
F32 = jnp.float32
PIECES = 1
BF16 = jnp.bfloat16


def reverse_bits(value, count):
    out = 0
    for bit in range(count):
        out = out | (((value >> bit) & 1) << (count - 1 - bit))
    return out


def block_tables(size):
    steps = jnp.arange(size, dtype=jnp.int32)
    turns = (4 * steps[None, :] + 1) * steps[:, None] % (4 * size)
    angle = (2.0 * math.pi / (4 * size)) * turns.astype(F32)
    cos, sin = jnp.cos(angle), jnp.sin(angle)

    def parts(table):
        high = table.astype(BF16)
        return high, (table - high.astype(F32)).astype(BF16)

    forward = jnp.concatenate([cos, -sin], axis=1)
    inverse = jnp.concatenate([cos.T, -sin.T], axis=0) / size
    return (
        jnp.concatenate(parts(forward), axis=0),
        jnp.concatenate(parts(inverse), axis=1),
    )


def matmul(left, right):
    return jnp.dot(left, right, preferred_element_type=F32)


def to_spectrum(rows, table):
    size = rows.shape[1]
    out = matmul(jnp.concatenate([rows, rows], axis=1), table)
    return out[:, :size], out[:, size:]


def from_spectrum(real, imag, table):
    size = real.shape[1]
    both = jnp.concatenate([real, imag], axis=1)
    high = both.astype(BF16)
    low = (both - high.astype(F32)).astype(BF16)
    out = matmul(high, table)
    return out[:, :size] + out[:, size:] + matmul(low, table[:, :size])


def split_rows(array, count):
    step = array.shape[0] // count
    return [array[i * step : (i + 1) * step] for i in range(count)]


def prepare_kernel(n, index_ref, *refs):
    given, (taps_ref, table_ref, inverse_ref) = refs[:n], refs[n : n + 3]
    grad_ref, filt_ref, tap_ref, filters, cotangents = refs[n + 3 :]
    s = index_ref[0]
    size = taps_ref.shape[1]
    for r in range(n):
        filters[s ^ r] = given[r][0]
        cotangents[s ^ r] = given[r][1]
    table = table_ref[...]
    filt_re, filt_im = to_spectrum(filters[...].reshape(n * size, size), table)
    cot_re, cot_im = to_spectrum(cotangents[...].reshape(n * size, size), table)
    filt_ref[:, :size] = filt_re
    filt_ref[:, size:] = filt_im
    taps = taps_ref[pl.ds(pl.multiple_of(s * size, size), size), :]
    taps_high = taps.astype(BF16)
    taps_low = (taps - taps_high.astype(F32)).astype(BF16)
    tap_re, tap_im = to_spectrum(taps_high, table)
    rest = matmul(taps_low, table[:size])
    tap_ref[:, :size] = tap_re + rest[:, :size]
    tap_ref[:, size:] = tap_im + rest[:, size:]
    fr, fi = split_rows(filt_re, n), split_rows(filt_im, n)
    cr, ci = split_rows(cot_re, n), split_rows(cot_im, n)
    turned = []
    for b in range(n):
        if b + 1 < n:
            turned.append((cr[b] + ci[b + 1], ci[b] - cr[b + 1]))
        else:
            turned.append((cr[b], ci[b]))
    real, imag = [], []
    for b in range(n):
        re, im = 0.0, 0.0
        for d in range(n - b):
            vr, vi = turned[b + d]
            re = re + fr[d] * vr + fi[d] * vi
            im = im + fr[d] * vi - fi[d] * vr
        real.append(re)
        imag.append(im)
    out = from_spectrum(jnp.concatenate(real), jnp.concatenate(imag), inverse_ref[...])
    grad_ref[...] = out.astype(BF16).reshape(n, size, size)


def gate_kernel(n, index_ref, *refs):
    blocks, refs = refs[:n], refs[n:]
    grad_in_ref, tap_ref, table_ref, inverse_ref = refs[:4]
    kept_ref, gated_ref, held, lent = refs[4], refs[5], refs[-1], refs[6:-1]
    c = index_ref[1]
    half, size = n // 2, tap_ref.shape[0]
    bits = n.bit_length() - 1
    for j in range(n):
        held[c ^ j] = blocks[j][...]
    values = held[...].reshape(n * size, size)
    table, inverse = table_ref[...], inverse_ref[...]
    tr, ti = tap_ref[:, :size], tap_ref[:, size:]
    wide = values.astype(F32)
    gate = 1.0 / (1.0 + jnp.exp(-wide))
    grad = grad_in_ref[...].reshape(n * size, size).astype(F32)
    grad_medium = (grad * gate).astype(BF16)
    re, im = to_spectrum(values, table)
    gr, gi = to_spectrum(grad_medium, table)
    re, im, gr, gi = (split_rows(x, n) for x in (re, im, gr, gi))
    real, imag, back_real, back_imag = [], [], [], []
    for b in range(n):
        ur, ui = (re[b] - im[b - 1], im[b] + re[b - 1]) if b else (re[b], im[b])
        real.append(tr * ur - ti * ui)
        imag.append(tr * ui + ti * ur)
        vr, vi = (gr[b] + gi[b + 1], gi[b] - gr[b + 1]) if b + 1 < n else (gr[b], gi[b])
        back_real.append(tr * vr + ti * vi)
        back_imag.append(tr * vi - ti * vr)
    medium = from_spectrum(jnp.concatenate(real), jnp.concatenate(imag), inverse)
    through = from_spectrum(jnp.concatenate(back_real), jnp.concatenate(back_imag), inverse)
    gated_ref[...] = (medium * gate).astype(BF16).reshape(n, size, size)
    back = (through + grad * medium * gate * (1.0 - gate)).astype(BF16)
    held[...] = back.reshape(n, size, size)
    for j in range(half):
        target = lent[j - 1] if j else kept_ref
        target[0] = held[reverse_bits(c ^ (half + j), bits)]
        target[1] = held[reverse_bits(c ^ j, bits)]


def long_kernel(n, index_ref, near_ref, gated_ref, filt_ref, table_ref, inverse_ref, *refs):
    outs, held = refs[:n], refs[n]
    s = index_ref[0]
    size = gated_ref.shape[2]
    re, im = to_spectrum(gated_ref[...].reshape(n * size, size), table_ref[...])
    re, im = split_rows(re, n), split_rows(im, n)
    fr, fi = split_rows(filt_ref[:, :size], n), split_rows(filt_ref[:, size:], n)
    turned = [(re[0], im[0])]
    for b in range(1, n):
        turned.append((re[b] - im[b - 1], im[b] + re[b - 1]))
    real, imag = [], []
    for b in range(n):
        zr, zi = 0.0, 0.0
        for d in range(b + 1):
            ur, ui = turned[b - d]
            zr = zr + fr[d] * ur - fi[d] * ui
            zi = zi + fr[d] * ui + fi[d] * ur
        real.append(zr)
        imag.append(zi)
    out = from_spectrum(jnp.concatenate(real), jnp.concatenate(imag), inverse_ref[...])
    held[...] = out.astype(BF16).reshape(n, size, size)
    for r in range(n):
        outs[r][: n // 2] = near_ref[...]
        outs[r][n // 2] = held[s ^ r]


def place_kernel(n, index_ref, *refs):
    given, out_ref = refs[:n], refs[n]
    s = index_ref[0]
    size = given[0].shape[1]
    for r in range(n):
        out_ref[pl.ds(pl.multiple_of((s ^ r) * size, size), size), :] = given[r][n // 2]


def arrange_kernel(n, index_ref, given_ref, filters_ref, cotangent_ref, *refs):
    weight_ref, turned_ref, blocks = refs[0], refs[1], refs[2:]
    s = index_ref[0]
    size = given_ref.shape[1] // n
    for r in range(n):
        start = pl.multiple_of((s ^ r) * size, size)
        blocks[r][0] = filters_ref[pl.ds(start, size), :]
        blocks[r][1] = cotangent_ref[pl.ds(start, size), :]
        block = given_ref[:, pl.ds(start, size)]
        weight_ref[:, r * size : (r + 1) * size] = block
        turned_ref[r * size : (r + 1) * size, :] = block.T


def values_kernel(n, *refs):
    half = n // 2
    weights, (upper_ref, lower_ref), outs = refs[:half], refs[half : half + 2], refs[half + 2 :]
    right = jnp.concatenate([upper_ref[...], lower_ref[...]], axis=0)
    step = weights[0].shape[0] // n
    for j in range(half):
        out = matmul(weights[j][...], right).astype(BF16)
        for r in range(n):
            outs[r][j] = out[r * step : (r + 1) * step]


def sum_kernel(n, *refs):
    terms, outs = refs[: -(n // 2)], refs[-(n // 2) :]
    for j, out_ref in enumerate(outs):
        total = terms[0][j].astype(F32)
        for term in terms[1:]:
            total = total + term[j].astype(F32)
        out_ref[...] = total.astype(BF16)


def input_kernel(n, *refs):
    half = n // 2
    weights, grads, outs = refs[:half], refs[half : half + n], refs[half + n :]
    total = 0.0
    for j in range(half):
        right = jnp.concatenate([ref[j] for ref in grads], axis=0)
        total = total + matmul(weights[j][...], right)
    rows = outs[0].shape[0]
    for k, out_ref in enumerate(outs):
        out_ref[...] = total[k * rows : (k + 1) * rows].astype(out_ref.dtype)


def total_kernel(k, near_ref, far_ref, out_ref):
    rows = far_ref.shape[0]
    near = near_ref[k * rows : (k + 1) * rows, :]
    out_ref[...] = (near + far_ref[...].astype(F32)).astype(BF16)


def cut_kernel(rows, given_ref, lower_ref, upper_ref, done):
    low = pltpu.make_async_copy(given_ref.at[rows:], lower_ref, done.at[0])
    high = pltpu.make_async_copy(given_ref.at[:rows], upper_ref, done.at[1])
    low.start()
    high.start()
    low.wait()
    high.wait()


def call(kernel, outs, scratch, index, args, flops, place=pltpu.VMEM):
    sizes = sum(math.prod(a.shape) * a.dtype.itemsize for a in (*args, *outs))
    held = sum(math.prod(a.shape) * 4 for a in scratch)
    specs = [pl.BlockSpec(memory_space=place)] * len(args)
    if index is not None:
        specs = [pl.BlockSpec(memory_space=pltpu.SMEM)] + specs
        args = (index, *args)
    return pl.pallas_call(
        kernel,
        out_shape=tuple(outs),
        in_specs=specs,
        out_specs=tuple(pl.BlockSpec(memory_space=pltpu.VMEM) for _ in outs),
        scratch_shapes=scratch,
        cost_estimate=pl.CostEstimate(flops=flops, bytes_accessed=sizes, transcendentals=0),
        compiler_params=pltpu.CompilerParams(vmem_limit_bytes=3 * (sizes + held) + (4 << 20)),
    )(*args)


def square_plan(n, activations, projection, medium_taps, long_filters, cotangent):
    bits = n.bit_length() - 1
    half = n // 2
    depth, size = activations.shape
    own = projection.shape[1] // n
    s, c = lax.axis_index("seq"), lax.axis_index("ch")
    index = jnp.stack([s, c]).astype(jnp.int32)
    shape = jax.ShapeDtypeStruct

    def move(array, target):
        pairs = [
            (i * n + j, (lambda t: t[0] * n + t[1])(target(i, j)))
            for i in range(n)
            for j in range(n)
        ]
        return lax.ppermute(array, ("seq", "ch"), pairs)

    def across_seq(array, step):
        return move(array, lambda i, j: (i ^ step, j))

    def across_ch(array, r):
        return move(array, lambda i, j: (i, j ^ r))

    def spread(parts):
        return [parts[0]] + [across_seq(parts[r], r) for r in range(1, n)]

    def share_seq(part):
        held, step = {0: part}, n // 2
        while step:
            for r in list(held):
                held[r | step] = across_seq(held[r], step)
            step //= 2
        return [held[r] for r in range(n)]

    def lend(parts):
        return [parts[0]] + [across_ch(parts[j], j) for j in range(1, half)]

    low_rows = 3 * depth // 8
    lower, upper = call(
        functools.partial(cut_kernel, depth - low_rows),
        [shape((low_rows, size), BF16), shape((depth - low_rows, size), BF16)],
        [pltpu.SemaphoreType.DMA((2,))],
        None,
        (activations,),
        0,
        place=pl.ANY,
    )
    moved = across_ch(lower, half)
    upper = move(upper, lambda i, j: (j, i))
    lower = move(moved, lambda i, j: (j ^ half, i))
    weight, weight_t, *blocks = call(
        functools.partial(arrange_kernel, n),
        [shape(projection.shape, BF16), shape(projection.shape[::-1], BF16)]
        + [shape((2, own, size), BF16)] * n,
        [],
        index,
        (projection, long_filters, cotangent),
        0,
    )
    table, inverse = block_tables(size)
    weight, weight_t, table, inverse, *blocks = lax.optimization_barrier(
        (weight, weight_t, table, inverse, *blocks)
    )

    weights, weights_t = lend([weight] * half), lend([weight_t] * half)

    def values_of(upper, lower):
        parts = call(
            functools.partial(values_kernel, n),
            [shape((half, own, size), BF16)] * n,
            [],
            None,
            (*weights_t, upper, lower),
            2 * depth * n * own * half * size,
        )
        terms = spread(parts)
        sums = call(
            functools.partial(sum_kernel, n),
            [shape((own, size), BF16)] * half,
            [],
            None,
            tuple(terms),
            n * half * own * size,
        )
        return lend(sums)

    far_upper, far_lower = across_ch(upper, half), across_ch(lower, half)
    blocks = spread(blocks)
    near_values = values_of(upper, lower)
    far_values = values_of(far_upper, far_lower)

    spectrum = 4 * n * size * 2 * size * own
    grad_gated, filt, tap = call(
        functools.partial(prepare_kernel, n),
        [shape((n, own, size), BF16), shape((n * own, 2 * size), F32), shape((own, 2 * size), F32)],
        [pltpu.VMEM((n, own, size), BF16), pltpu.VMEM((n, own, size), BF16)],
        index,
        (*blocks, medium_taps, table, inverse),
        6 * spectrum,
    )
    kept, gated, *lent = call(
        functools.partial(gate_kernel, n),
        [shape((2, own, size), BF16), shape((n, own, size), BF16)]
        + [shape((2, own, size), BF16)] * (half - 1),
        [pltpu.VMEM((n, own, size), BF16)],
        index,
        (*near_values, *far_values, grad_gated, tap, table, inverse),
        8 * spectrum,
    )
    pairs = lend([kept, *lent])
    far_back = share_seq(jnp.stack([pair[0] for pair in pairs]))
    near = jnp.stack([pair[1] for pair in pairs])

    near_back = call(
        functools.partial(long_kernel, n),
        [shape((half + 1, own, size), BF16)] * n,
        [pltpu.VMEM((n, own, size), BF16)],
        index,
        (near, gated, filt, table, inverse),
        4 * spectrum,
    )
    near_back = spread(near_back)

    def input_of(parts, kind, pieces):
        return call(
            functools.partial(input_kernel, n),
            [shape((depth // pieces, size), kind)] * pieces,
            [],
            None,
            (*weights, *parts),
            2 * depth * n * own * half * size,
        )

    far_total = input_of(far_back, BF16, PIECES)
    (near_total,) = input_of(near_back, F32, 1)
    homes = []
    for k in range(PIECES):
        moved = across_ch(far_total[k], half)
        (total,) = call(
            functools.partial(total_kernel, k),
            [shape((depth // PIECES, size), BF16)],
            [],
            None,
            (near_total, moved),
            depth // PIECES * size,
        )
        homes.append(move(total, lambda i, j: (reverse_bits(j, bits), i)))
    input_grad = jnp.concatenate(homes) if PIECES > 1 else homes[0]
    (conv_out,) = call(
        functools.partial(place_kernel, n),
        [shape((n * own, size), BF16)],
        [],
        index,
        tuple(near_back),
        0,
    )
    return conv_out, input_grad


def medium_forward(padded, tap_weights, length):
    tap_count = tap_weights.shape[1]
    summed = jnp.zeros((padded.shape[0], length), jnp.float32)
    for offset in range(tap_count):
        begin_col = tap_count - 1 - offset
        summed = (
            summed + tap_weights[:, offset : offset + 1] * padded[:, begin_col : begin_col + length]
        )
    return summed


def medium_backward(padded, tap_weights, length):
    tap_count = tap_weights.shape[1]
    summed = jnp.zeros((padded.shape[0], length), jnp.float32)
    for offset in range(tap_count):
        summed = summed + tap_weights[:, offset : offset + 1] * padded[:, offset : offset + length]
    return summed


def dft_tables(length):
    points = 2 * length
    columns = 128
    row_count = points // columns
    half_rows = row_count // 2
    freq_rows = jnp.arange(row_count, dtype=jnp.int32)
    time_rows = jnp.arange(half_rows, dtype=jnp.int32)
    lane_index = jnp.arange(columns, dtype=jnp.int32)
    angle_first = (
        2.0
        * math.pi
        / row_count
        * (freq_rows[:, None] * time_rows[None, :] % row_count).astype(jnp.float32)
    )
    angle_twist = (
        2.0
        * math.pi
        / points
        * (freq_rows[:, None] * lane_index[None, :] % points).astype(jnp.float32)
    )
    angle_last = (
        2.0
        * math.pi
        / columns
        * (lane_index[:, None] * lane_index[None, :] % columns).astype(jnp.float32)
    )
    return (
        jnp.cos(angle_first),
        jnp.sin(angle_first),
        jnp.cos(angle_twist),
        jnp.sin(angle_twist),
        jnp.cos(angle_last),
        jnp.sin(angle_last),
    )


def forward_dft(signal, tables):
    cos_first, sin_first, cos_twist, sin_twist, cos_last, sin_last = tables
    channels = signal.shape[0]
    shaped = signal.reshape(channels, cos_first.shape[1], 128)
    section_re = jnp.einsum("kn,cnq->ckq", cos_first, shaped, precision=exact_mode)
    section_im = -jnp.einsum("kn,cnq->ckq", sin_first, shaped, precision=exact_mode)
    twist_re = section_re * cos_twist + section_im * sin_twist
    twist_im = section_im * cos_twist - section_re * sin_twist
    spec_re = jnp.einsum("ckq,qm->ckm", twist_re, cos_last, precision=exact_mode) + jnp.einsum(
        "ckq,qm->ckm", twist_im, sin_last, precision=exact_mode
    )
    spec_im = jnp.einsum("ckq,qm->ckm", twist_im, cos_last, precision=exact_mode) - jnp.einsum(
        "ckq,qm->ckm", twist_re, sin_last, precision=exact_mode
    )
    return (spec_re, spec_im)


def inverse_dft(spec_re, spec_im, tables):
    cos_first, sin_first, cos_twist, sin_twist, cos_last, sin_last = tables
    channels = spec_re.shape[0]
    half_rows = cos_first.shape[1]
    inner_re = jnp.einsum("ckq,qm->ckm", spec_re, cos_last, precision=exact_mode) - jnp.einsum(
        "ckq,qm->ckm", spec_im, sin_last, precision=exact_mode
    )
    inner_im = jnp.einsum("ckq,qm->ckm", spec_im, cos_last, precision=exact_mode) + jnp.einsum(
        "ckq,qm->ckm", spec_re, sin_last, precision=exact_mode
    )
    turned_re = inner_re * cos_twist - inner_im * sin_twist
    turned_im = inner_im * cos_twist + inner_re * sin_twist
    output = jnp.einsum("kn,ckq->cnq", cos_first, turned_re, precision=exact_mode) - jnp.einsum(
        "kn,ckq->cnq", sin_first, turned_im, precision=exact_mode
    )
    points = 2 * half_rows * 128
    return (output / points).reshape(channels, half_rows * 128)


def causal_apply(signal, filt_re, filt_im, tables, conjugate):
    sig_re, sig_im = forward_dft(signal, tables)
    if conjugate:
        prod_re = sig_re * filt_re + sig_im * filt_im
        prod_im = sig_im * filt_re - sig_re * filt_im
    else:
        prod_re = sig_re * filt_re - sig_im * filt_im
        prod_im = sig_im * filt_re + sig_re * filt_im
    return inverse_dft(prod_re, prod_im, tables)


def on_device(activations, projection, medium_taps, long_filters, cotangent):
    tap_count = medium_taps.shape[1]
    whole_in = lax.all_gather(activations, "ch", axis=0, tiled=True)
    mixed_sum = lax.dot_general(
        lax.all_gather(projection, "seq", axis=0, tiled=True),
        whole_in,
        (((0,), (0,)), ((), ())),
        preferred_element_type=jnp.float32,
    )
    values = mixed_sum.astype(jnp.bfloat16)
    channel_count = values.shape[0] // lax.axis_size("seq")
    own_taps = lax.dynamic_slice_in_dim(
        medium_taps, lax.axis_index("seq") * channel_count, channel_count, 0
    )
    arrived, filters_ch = (
        lax.all_to_all(values, "seq", split_axis=0, concat_axis=1, tiled=True),
        lax.all_to_all(long_filters, "seq", split_axis=0, concat_axis=1, tiled=True),
    )
    tables = dft_tables(arrived.shape[1])
    filt_re, filt_im = forward_dft(filters_ch.astype(jnp.float32), tables)
    values_ch = arrived.astype(jnp.float32)
    padded_ch = jnp.pad(values_ch, ((0, 0), (tap_count - 1, 0)))
    conv_ch = medium_forward(padded_ch, own_taps, arrived.shape[1])
    gate_ch = jax.nn.sigmoid(values_ch)
    signal = lax.optimization_barrier((conv_ch * gate_ch).astype(jnp.bfloat16)).astype(jnp.float32)
    kept_state = (conv_ch, gate_ch)
    output_ch = causal_apply(signal, filt_re, filt_im, tables, False).astype(jnp.bfloat16)
    output_ch, context = (output_ch, (filt_re, filt_im, tables, kept_state))
    conv_out = lax.all_to_all(output_ch, "seq", split_axis=1, concat_axis=0, tiled=True)
    grad_ch = lax.all_to_all(cotangent, "seq", split_axis=0, concat_axis=1, tiled=True)
    filt_re, filt_im, tables, kept_state = context
    back_grad = lax.optimization_barrier(
        causal_apply(grad_ch.astype(jnp.float32), filt_re, filt_im, tables, True).astype(
            jnp.bfloat16
        )
    )
    conv_ch, gate_ch = kept_state
    grad_wide = back_grad.astype(jnp.float32)
    conv_grad = lax.optimization_barrier((grad_wide * gate_ch).astype(jnp.bfloat16)).astype(
        jnp.float32
    )
    padded_grad = jnp.pad(conv_grad, ((0, 0), (0, tap_count - 1)))
    through = medium_backward(padded_grad, own_taps, conv_grad.shape[1])
    gate_grad = grad_wide * conv_ch * gate_ch * (1.0 - gate_ch)
    back_ch = (through + gate_grad).astype(jnp.bfloat16)
    returned = lax.all_to_all(back_ch, "seq", split_axis=1, concat_axis=0, tiled=True)
    partial_grad = jnp.dot(
        lax.all_gather(projection, "seq", axis=0, tiled=True),
        returned,
        preferred_element_type=jnp.float32,
    )
    input_grad = lax.psum_scatter(
        partial_grad.astype(jnp.bfloat16), "ch", scatter_dimension=0, tiled=True
    )
    return (conv_out, input_grad)


def fits_square(mesh, activations, projection, medium_taps):
    seq, ch = mesh.shape["seq"], mesh.shape["ch"]
    size = activations.shape[1] // (mesh.shape["grp"] * seq)
    return (
        seq == ch
        and seq > 1
        and seq & (seq - 1) == 0
        and medium_taps.shape[1] == size
        and projection.shape[1] == seq * ch * size
        and size % 128 == 0
        and activations.shape[0] % (2 * ch * size) == 0
    )


def solution(mesh):
    n = mesh.shape["seq"]

    def placed(body):
        return jax.shard_map(
            body,
            mesh=mesh,
            in_specs=(
                P("ch", ("grp", "seq")),
                P("seq", "ch"),
                P("ch", None),
                P("ch", "seq"),
                P("ch", ("grp", "seq")),
            ),
            out_specs=(P("ch", ("grp", "seq")), P("ch", ("grp", "seq"))),
            check_vma=False,
        )

    def square(*args):
        return square_plan(n, *args)

    def step(*args):
        return placed(square if fits_square(mesh, *args[:3]) else on_device)(*args)

    if mesh.shape["seq"] != mesh.shape["ch"]:
        return step
    return step
```

```python
import functools
import math

import jax
import jax.numpy as jnp
from jax import lax
from jax.experimental import pallas as pl
from jax.experimental.pallas import tpu as pltpu
from jax.sharding import PartitionSpec as P


exact_mode = lax.Precision.HIGH
F32 = jnp.float32
PIECES = 1
BF16 = jnp.bfloat16


def reverse_bits(value, count):
    out = 0
    for bit in range(count):
        out = out | (((value >> bit) & 1) << (count - 1 - bit))
    return out


def block_tables(size):
    steps = jnp.arange(size, dtype=jnp.int32)
    turns = (4 * steps[None, :] + 1) * steps[:, None] % (4 * size)
    angle = (2.0 * math.pi / (4 * size)) * turns.astype(F32)
    cos, sin = jnp.cos(angle), jnp.sin(angle)

    def parts(table):
        high = table.astype(BF16)
        return high, (table - high.astype(F32)).astype(BF16)

    forward = jnp.concatenate([cos, -sin], axis=1)
    inverse = jnp.concatenate([cos.T, -sin.T], axis=0) / size
    return (
        jnp.concatenate(parts(forward), axis=0),
        jnp.concatenate(parts(inverse), axis=1),
    )


def matmul(left, right):
    return jnp.dot(left, right, preferred_element_type=F32)


def to_spectrum(rows, table):
    size = rows.shape[1]
    out = matmul(jnp.concatenate([rows, rows], axis=1), table)
    return out[:, :size], out[:, size:]


def from_spectrum(real, imag, table):
    size = real.shape[1]
    both = jnp.concatenate([real, imag], axis=1)
    high = both.astype(BF16)
    low = (both - high.astype(F32)).astype(BF16)
    out = matmul(high, table)
    return out[:, :size] + out[:, size:] + matmul(low, table[:, :size])


def split_rows(array, count):
    step = array.shape[0] // count
    return [array[i * step : (i + 1) * step] for i in range(count)]


def prepare_kernel(n, index_ref, *refs):
    given, (taps_ref, table_ref, inverse_ref) = refs[:n], refs[n : n + 3]
    grad_ref, filt_ref, tap_ref, filters, cotangents = refs[n + 3 :]
    s = index_ref[0]
    size = taps_ref.shape[1]
    for r in range(n):
        filters[s ^ r] = given[r][0]
        cotangents[s ^ r] = given[r][1]
    table = table_ref[...]
    filt_re, filt_im = to_spectrum(filters[...].reshape(n * size, size), table)
    cot_re, cot_im = to_spectrum(cotangents[...].reshape(n * size, size), table)
    filt_ref[:, :size] = filt_re
    filt_ref[:, size:] = filt_im
    taps = taps_ref[pl.ds(pl.multiple_of(s * size, size), size), :]
    taps_high = taps.astype(BF16)
    taps_low = (taps - taps_high.astype(F32)).astype(BF16)
    tap_re, tap_im = to_spectrum(taps_high, table)
    rest = matmul(taps_low, table[:size])
    tap_ref[:, :size] = tap_re + rest[:, :size]
    tap_ref[:, size:] = tap_im + rest[:, size:]
    fr, fi = split_rows(filt_re, n), split_rows(filt_im, n)
    cr, ci = split_rows(cot_re, n), split_rows(cot_im, n)
    turned = []
    for b in range(n):
        if b + 1 < n:
            turned.append((cr[b] + ci[b + 1], ci[b] - cr[b + 1]))
        else:
            turned.append((cr[b], ci[b]))
    real, imag = [], []
    for b in range(n):
        re, im = 0.0, 0.0
        for d in range(n - b):
            vr, vi = turned[b + d]
            re = re + fr[d] * vr + fi[d] * vi
            im = im + fr[d] * vi - fi[d] * vr
        real.append(re)
        imag.append(im)
    out = from_spectrum(jnp.concatenate(real), jnp.concatenate(imag), inverse_ref[...])
    grad_ref[...] = out.astype(BF16).reshape(n, size, size)


def gate_kernel(n, index_ref, *refs):
    blocks, refs = refs[:n], refs[n:]
    grad_in_ref, tap_ref, table_ref, inverse_ref = refs[:4]
    kept_ref, gated_ref, held, lent = refs[4], refs[5], refs[-1], refs[6:-1]
    c = index_ref[1]
    half, size = n // 2, tap_ref.shape[0]
    bits = n.bit_length() - 1
    for j in range(n):
        held[c ^ j ^ half] = blocks[j][...]
    values = held[...].reshape(n * size, size)
    table, inverse = table_ref[...], inverse_ref[...]
    tr, ti = tap_ref[:, :size], tap_ref[:, size:]
    wide = values.astype(F32)
    gate = 1.0 / (1.0 + jnp.exp(-wide))
    grad = grad_in_ref[...].reshape(n * size, size).astype(F32)
    grad_medium = (grad * gate).astype(BF16)
    re, im = to_spectrum(values, table)
    gr, gi = to_spectrum(grad_medium, table)
    re, im, gr, gi = (split_rows(x, n) for x in (re, im, gr, gi))
    real, imag, back_real, back_imag = [], [], [], []
    for b in range(n):
        ur, ui = (re[b] - im[b - 1], im[b] + re[b - 1]) if b else (re[b], im[b])
        real.append(tr * ur - ti * ui)
        imag.append(tr * ui + ti * ur)
        vr, vi = (gr[b] + gi[b + 1], gi[b] - gr[b + 1]) if b + 1 < n else (gr[b], gi[b])
        back_real.append(tr * vr + ti * vi)
        back_imag.append(tr * vi - ti * vr)
    medium = from_spectrum(jnp.concatenate(real), jnp.concatenate(imag), inverse)
    through = from_spectrum(jnp.concatenate(back_real), jnp.concatenate(back_imag), inverse)
    gated_ref[...] = (medium * gate).astype(BF16).reshape(n, size, size)
    back = (through + grad * medium * gate * (1.0 - gate)).astype(BF16)
    held[...] = back.reshape(n, size, size)
    for j in range(half):
        target = lent[j - 1] if j else kept_ref
        target[0] = held[reverse_bits(c ^ (half + j) ^ half, bits)]
        target[1] = held[reverse_bits(c ^ j ^ half, bits)]


def long_kernel(n, index_ref, near_ref, gated_ref, filt_ref, table_ref, inverse_ref, *refs):
    outs, held = refs[:n], refs[n]
    s = index_ref[0]
    size = gated_ref.shape[2]
    re, im = to_spectrum(gated_ref[...].reshape(n * size, size), table_ref[...])
    re, im = split_rows(re, n), split_rows(im, n)
    fr, fi = split_rows(filt_ref[:, :size], n), split_rows(filt_ref[:, size:], n)
    turned = [(re[0], im[0])]
    for b in range(1, n):
        turned.append((re[b] - im[b - 1], im[b] + re[b - 1]))
    real, imag = [], []
    for b in range(n):
        zr, zi = 0.0, 0.0
        for d in range(b + 1):
            ur, ui = turned[b - d]
            zr = zr + fr[d] * ur - fi[d] * ui
            zi = zi + fr[d] * ui + fi[d] * ur
        real.append(zr)
        imag.append(zi)
    out = from_spectrum(jnp.concatenate(real), jnp.concatenate(imag), inverse_ref[...])
    held[...] = out.astype(BF16).reshape(n, size, size)
    for r in range(n):
        outs[r][: n // 2] = near_ref[...]
        outs[r][n // 2] = held[s ^ r]


def place_kernel(n, index_ref, *refs):
    given, out_ref = refs[:n], refs[n]
    s = index_ref[0]
    size = given[0].shape[1]
    for r in range(n):
        out_ref[pl.ds(pl.multiple_of((s ^ r) * size, size), size), :] = given[r][n // 2]


def arrange_kernel(n, index_ref, given_ref, filters_ref, cotangent_ref, *refs):
    weight_ref, turned_ref, blocks = refs[0], refs[1], refs[2:]
    s = index_ref[0]
    size = given_ref.shape[1] // n
    for r in range(n):
        start = pl.multiple_of((s ^ r) * size, size)
        blocks[r][0] = filters_ref[pl.ds(start, size), :]
        blocks[r][1] = cotangent_ref[pl.ds(start, size), :]
        block = given_ref[:, pl.ds(start, size)]
        weight_ref[:, r * size : (r + 1) * size] = block
        turned_ref[r * size : (r + 1) * size, :] = block.T


def values_kernel(n, *refs):
    half = n // 2
    weights, (upper_ref, lower_ref), outs = refs[:half], refs[half : half + 2], refs[half + 2 :]
    right = jnp.concatenate([upper_ref[...], lower_ref[...]], axis=0)
    step = weights[0].shape[0] // n
    for j in range(half):
        out = matmul(weights[j][...], right).astype(BF16)
        for r in range(n):
            outs[r][j] = out[r * step : (r + 1) * step]


def sum_kernel(n, *refs):
    terms, outs = refs[: -(n // 2)], refs[-(n // 2) :]
    for j, out_ref in enumerate(outs):
        total = terms[0][j].astype(F32)
        for term in terms[1:]:
            total = total + term[j].astype(F32)
        out_ref[...] = total.astype(BF16)


def input_kernel(n, *refs):
    half = n // 2
    weights, grads, outs = refs[:half], refs[half : half + n], refs[half + n :]
    total = 0.0
    for j in range(half):
        right = jnp.concatenate([ref[j] for ref in grads], axis=0)
        total = total + matmul(weights[j][...], right)
    rows = outs[0].shape[0]
    for k, out_ref in enumerate(outs):
        out_ref[...] = total[k * rows : (k + 1) * rows].astype(out_ref.dtype)


def total_kernel(k, near_ref, far_ref, out_ref):
    rows = far_ref.shape[0]
    near = near_ref[k * rows : (k + 1) * rows, :]
    out_ref[...] = (near + far_ref[...].astype(F32)).astype(BF16)


def cut_kernel(rows, given_ref, lower_ref, upper_ref, done):
    low = pltpu.make_async_copy(given_ref.at[rows:], lower_ref, done.at[0])
    high = pltpu.make_async_copy(given_ref.at[:rows], upper_ref, done.at[1])
    low.start()
    high.start()
    low.wait()
    high.wait()


def call(kernel, outs, scratch, index, args, flops, place=pltpu.VMEM):
    sizes = sum(math.prod(a.shape) * a.dtype.itemsize for a in (*args, *outs))
    held = sum(math.prod(a.shape) * 4 for a in scratch)
    specs = [pl.BlockSpec(memory_space=place)] * len(args)
    if index is not None:
        specs = [pl.BlockSpec(memory_space=pltpu.SMEM)] + specs
        args = (index, *args)
    return pl.pallas_call(
        kernel,
        out_shape=tuple(outs),
        in_specs=specs,
        out_specs=tuple(pl.BlockSpec(memory_space=pltpu.VMEM) for _ in outs),
        scratch_shapes=scratch,
        cost_estimate=pl.CostEstimate(flops=flops, bytes_accessed=sizes, transcendentals=0),
        compiler_params=pltpu.CompilerParams(vmem_limit_bytes=3 * (sizes + held) + (4 << 20)),
    )(*args)


def square_plan(n, activations, projection, medium_taps, long_filters, cotangent):
    bits = n.bit_length() - 1
    half = n // 2
    depth, size = activations.shape
    own = projection.shape[1] // n
    s, c = lax.axis_index("seq"), lax.axis_index("ch")
    index = jnp.stack([s, c]).astype(jnp.int32)
    shape = jax.ShapeDtypeStruct

    def move(array, target):
        pairs = [
            (i * n + j, (lambda t: t[0] * n + t[1])(target(i, j)))
            for i in range(n)
            for j in range(n)
        ]
        return lax.ppermute(array, ("seq", "ch"), pairs)

    def across_seq(array, step):
        return move(array, lambda i, j: (i ^ step, j))

    def across_ch(array, r):
        return move(array, lambda i, j: (i, j ^ r))

    def spread(parts):
        return [parts[0]] + [across_seq(parts[r], r) for r in range(1, n)]

    def lend(parts):
        return [parts[0]] + [across_ch(parts[j], j) for j in range(1, half)]

    low_rows = depth // 8
    lower, upper = call(
        functools.partial(cut_kernel, depth - low_rows),
        [shape((low_rows, size), BF16), shape((depth - low_rows, size), BF16)],
        [pltpu.SemaphoreType.DMA((2,))],
        None,
        (activations,),
        0,
        place=pl.ANY,
    )
    moved = across_ch(lower, half)
    upper = move(upper, lambda i, j: (j, i ^ half))
    lower = move(moved, lambda i, j: (j ^ half, i ^ half))
    weight, weight_t, *blocks = call(
        functools.partial(arrange_kernel, n),
        [shape(projection.shape, BF16), shape(projection.shape[::-1], BF16)]
        + [shape((2, own, size), BF16)] * n,
        [],
        index,
        (projection, long_filters, cotangent),
        0,
    )
    table, inverse = block_tables(size)
    weight, weight_t, table, inverse, *blocks = lax.optimization_barrier(
        (weight, weight_t, table, inverse, *blocks)
    )

    weights, weights_t = lend([weight] * half), lend([weight_t] * half)

    def values_of(upper, lower):
        parts = call(
            functools.partial(values_kernel, n),
            [shape((half, own, size), BF16)] * n,
            [],
            None,
            (*weights_t, upper, lower),
            2 * depth * n * own * half * size,
        )
        terms = spread(parts)
        sums = call(
            functools.partial(sum_kernel, n),
            [shape((own, size), BF16)] * half,
            [],
            None,
            tuple(terms),
            n * half * own * size,
        )
        return lend(sums)

    far_upper, far_lower = across_ch(upper, half), across_ch(lower, half)
    blocks = spread(blocks)
    near_values = values_of(upper, lower)
    far_values = values_of(far_upper, far_lower)

    spectrum = 4 * n * size * 2 * size * own
    grad_gated, filt, tap = call(
        functools.partial(prepare_kernel, n),
        [shape((n, own, size), BF16), shape((n * own, 2 * size), F32), shape((own, 2 * size), F32)],
        [pltpu.VMEM((n, own, size), BF16), pltpu.VMEM((n, own, size), BF16)],
        index,
        (*blocks, medium_taps, table, inverse),
        6 * spectrum,
    )
    kept, gated, *lent = call(
        functools.partial(gate_kernel, n),
        [shape((2, own, size), BF16), shape((n, own, size), BF16)]
        + [shape((2, own, size), BF16)] * (half - 1),
        [pltpu.VMEM((n, own, size), BF16)],
        index,
        (*near_values, *far_values, grad_gated, tap, table, inverse),
        8 * spectrum,
    )
    pairs = lend([kept, *lent])
    far = jnp.stack([pair[0] for pair in pairs])
    far_back = spread([far] * n)
    near = jnp.stack([pair[1] for pair in pairs])

    near_back = call(
        functools.partial(long_kernel, n),
        [shape((half + 1, own, size), BF16)] * n,
        [pltpu.VMEM((n, own, size), BF16)],
        index,
        (near, gated, filt, table, inverse),
        4 * spectrum,
    )
    near_back = spread(near_back)

    def input_of(parts, kind, pieces):
        return call(
            functools.partial(input_kernel, n),
            [shape((depth // pieces, size), kind)] * pieces,
            [],
            None,
            (*weights, *parts),
            2 * depth * n * own * half * size,
        )

    far_total = input_of(far_back, BF16, PIECES)
    (near_total,) = input_of(near_back, F32, 1)
    homes = []
    for k in range(PIECES):
        moved = across_ch(far_total[k], half)
        (total,) = call(
            functools.partial(total_kernel, k),
            [shape((depth // PIECES, size), BF16)],
            [],
            None,
            (near_total, moved),
            depth // PIECES * size,
        )
        homes.append(move(total, lambda i, j: (reverse_bits(j ^ half, bits), i)))
    input_grad = jnp.concatenate(homes) if PIECES > 1 else homes[0]
    (conv_out,) = call(
        functools.partial(place_kernel, n),
        [shape((n * own, size), BF16)],
        [],
        index,
        tuple(near_back),
        0,
    )
    return conv_out, input_grad


def medium_forward(padded, tap_weights, length):
    tap_count = tap_weights.shape[1]
    summed = jnp.zeros((padded.shape[0], length), jnp.float32)
    for offset in range(tap_count):
        begin_col = tap_count - 1 - offset
        summed = (
            summed + tap_weights[:, offset : offset + 1] * padded[:, begin_col : begin_col + length]
        )
    return summed


def medium_backward(padded, tap_weights, length):
    tap_count = tap_weights.shape[1]
    summed = jnp.zeros((padded.shape[0], length), jnp.float32)
    for offset in range(tap_count):
        summed = summed + tap_weights[:, offset : offset + 1] * padded[:, offset : offset + length]
    return summed


def dft_tables(length):
    points = 2 * length
    columns = 128
    row_count = points // columns
    half_rows = row_count // 2
    freq_rows = jnp.arange(row_count, dtype=jnp.int32)
    time_rows = jnp.arange(half_rows, dtype=jnp.int32)
    lane_index = jnp.arange(columns, dtype=jnp.int32)
    angle_first = (
        2.0
        * math.pi
        / row_count
        * (freq_rows[:, None] * time_rows[None, :] % row_count).astype(jnp.float32)
    )
    angle_twist = (
        2.0
        * math.pi
        / points
        * (freq_rows[:, None] * lane_index[None, :] % points).astype(jnp.float32)
    )
    angle_last = (
        2.0
        * math.pi
        / columns
        * (lane_index[:, None] * lane_index[None, :] % columns).astype(jnp.float32)
    )
    return (
        jnp.cos(angle_first),
        jnp.sin(angle_first),
        jnp.cos(angle_twist),
        jnp.sin(angle_twist),
        jnp.cos(angle_last),
        jnp.sin(angle_last),
    )


def forward_dft(signal, tables):
    cos_first, sin_first, cos_twist, sin_twist, cos_last, sin_last = tables
    channels = signal.shape[0]
    shaped = signal.reshape(channels, cos_first.shape[1], 128)
    section_re = jnp.einsum("kn,cnq->ckq", cos_first, shaped, precision=exact_mode)
    section_im = -jnp.einsum("kn,cnq->ckq", sin_first, shaped, precision=exact_mode)
    twist_re = section_re * cos_twist + section_im * sin_twist
    twist_im = section_im * cos_twist - section_re * sin_twist
    spec_re = jnp.einsum("ckq,qm->ckm", twist_re, cos_last, precision=exact_mode) + jnp.einsum(
        "ckq,qm->ckm", twist_im, sin_last, precision=exact_mode
    )
    spec_im = jnp.einsum("ckq,qm->ckm", twist_im, cos_last, precision=exact_mode) - jnp.einsum(
        "ckq,qm->ckm", twist_re, sin_last, precision=exact_mode
    )
    return (spec_re, spec_im)


def inverse_dft(spec_re, spec_im, tables):
    cos_first, sin_first, cos_twist, sin_twist, cos_last, sin_last = tables
    channels = spec_re.shape[0]
    half_rows = cos_first.shape[1]
    inner_re = jnp.einsum("ckq,qm->ckm", spec_re, cos_last, precision=exact_mode) - jnp.einsum(
        "ckq,qm->ckm", spec_im, sin_last, precision=exact_mode
    )
    inner_im = jnp.einsum("ckq,qm->ckm", spec_im, cos_last, precision=exact_mode) + jnp.einsum(
        "ckq,qm->ckm", spec_re, sin_last, precision=exact_mode
    )
    turned_re = inner_re * cos_twist - inner_im * sin_twist
    turned_im = inner_im * cos_twist + inner_re * sin_twist
    output = jnp.einsum("kn,ckq->cnq", cos_first, turned_re, precision=exact_mode) - jnp.einsum(
        "kn,ckq->cnq", sin_first, turned_im, precision=exact_mode
    )
    points = 2 * half_rows * 128
    return (output / points).reshape(channels, half_rows * 128)


def causal_apply(signal, filt_re, filt_im, tables, conjugate):
    sig_re, sig_im = forward_dft(signal, tables)
    if conjugate:
        prod_re = sig_re * filt_re + sig_im * filt_im
        prod_im = sig_im * filt_re - sig_re * filt_im
    else:
        prod_re = sig_re * filt_re - sig_im * filt_im
        prod_im = sig_im * filt_re + sig_re * filt_im
    return inverse_dft(prod_re, prod_im, tables)


def on_device(activations, projection, medium_taps, long_filters, cotangent):
    tap_count = medium_taps.shape[1]
    whole_in = lax.all_gather(activations, "ch", axis=0, tiled=True)
    mixed_sum = lax.dot_general(
        lax.all_gather(projection, "seq", axis=0, tiled=True),
        whole_in,
        (((0,), (0,)), ((), ())),
        preferred_element_type=jnp.float32,
    )
    values = mixed_sum.astype(jnp.bfloat16)
    channel_count = values.shape[0] // lax.axis_size("seq")
    own_taps = lax.dynamic_slice_in_dim(
        medium_taps, lax.axis_index("seq") * channel_count, channel_count, 0
    )
    arrived, filters_ch = (
        lax.all_to_all(values, "seq", split_axis=0, concat_axis=1, tiled=True),
        lax.all_to_all(long_filters, "seq", split_axis=0, concat_axis=1, tiled=True),
    )
    tables = dft_tables(arrived.shape[1])
    filt_re, filt_im = forward_dft(filters_ch.astype(jnp.float32), tables)
    values_ch = arrived.astype(jnp.float32)
    padded_ch = jnp.pad(values_ch, ((0, 0), (tap_count - 1, 0)))
    conv_ch = medium_forward(padded_ch, own_taps, arrived.shape[1])
    gate_ch = jax.nn.sigmoid(values_ch)
    signal = lax.optimization_barrier((conv_ch * gate_ch).astype(jnp.bfloat16)).astype(jnp.float32)
    kept_state = (conv_ch, gate_ch)
    output_ch = causal_apply(signal, filt_re, filt_im, tables, False).astype(jnp.bfloat16)
    output_ch, context = (output_ch, (filt_re, filt_im, tables, kept_state))
    conv_out = lax.all_to_all(output_ch, "seq", split_axis=1, concat_axis=0, tiled=True)
    grad_ch = lax.all_to_all(cotangent, "seq", split_axis=0, concat_axis=1, tiled=True)
    filt_re, filt_im, tables, kept_state = context
    back_grad = lax.optimization_barrier(
        causal_apply(grad_ch.astype(jnp.float32), filt_re, filt_im, tables, True).astype(
            jnp.bfloat16
        )
    )
    conv_ch, gate_ch = kept_state
    grad_wide = back_grad.astype(jnp.float32)
    conv_grad = lax.optimization_barrier((grad_wide * gate_ch).astype(jnp.bfloat16)).astype(
        jnp.float32
    )
    padded_grad = jnp.pad(conv_grad, ((0, 0), (0, tap_count - 1)))
    through = medium_backward(padded_grad, own_taps, conv_grad.shape[1])
    gate_grad = grad_wide * conv_ch * gate_ch * (1.0 - gate_ch)
    back_ch = (through + gate_grad).astype(jnp.bfloat16)
    returned = lax.all_to_all(back_ch, "seq", split_axis=1, concat_axis=0, tiled=True)
    partial_grad = jnp.dot(
        lax.all_gather(projection, "seq", axis=0, tiled=True),
        returned,
        preferred_element_type=jnp.float32,
    )
    input_grad = lax.psum_scatter(
        partial_grad.astype(jnp.bfloat16), "ch", scatter_dimension=0, tiled=True
    )
    return (conv_out, input_grad)


def fits_square(mesh, activations, projection, medium_taps):
    seq, ch = mesh.shape["seq"], mesh.shape["ch"]
    size = activations.shape[1] // (mesh.shape["grp"] * seq)
    return (
        seq == ch
        and seq > 1
        and seq & (seq - 1) == 0
        and medium_taps.shape[1] == size
        and projection.shape[1] == seq * ch * size
        and size % 128 == 0
        and activations.shape[0] % (2 * ch * size) == 0
    )


def solution(mesh):
    n = mesh.shape["seq"]

    def placed(body):
        return jax.shard_map(
            body,
            mesh=mesh,
            in_specs=(
                P("ch", ("grp", "seq")),
                P("seq", "ch"),
                P("ch", None),
                P("ch", "seq"),
                P("ch", ("grp", "seq")),
            ),
            out_specs=(P("ch", ("grp", "seq")), P("ch", ("grp", "seq"))),
            check_vma=False,
        )

    def square(*args):
        return square_plan(n, *args)

    def step(*args):
        return placed(square if fits_square(mesh, *args[:3]) else on_device)(*args)

    if mesh.shape["seq"] != mesh.shape["ch"]:
        return step
    return step
```

```python
import functools
import math

import jax
import jax.numpy as jnp
from jax import lax
from jax.experimental import pallas as pl
from jax.experimental.pallas import tpu as pltpu
from jax.sharding import PartitionSpec as P


exact_mode = lax.Precision.HIGH
F32 = jnp.float32
PIECES = 1
BF16 = jnp.bfloat16


def reverse_bits(value, count):
    out = 0
    for bit in range(count):
        out = out | (((value >> bit) & 1) << (count - 1 - bit))
    return out


def block_tables(size):
    steps = jnp.arange(size, dtype=jnp.int32)
    turns = (4 * steps[None, :] + 1) * steps[:, None] % (4 * size)
    angle = (2.0 * math.pi / (4 * size)) * turns.astype(F32)
    cos, sin = jnp.cos(angle), jnp.sin(angle)

    def parts(table):
        high = table.astype(BF16)
        return high, (table - high.astype(F32)).astype(BF16)

    forward = jnp.concatenate([cos, -sin], axis=1)
    inverse = jnp.concatenate([cos.T, -sin.T], axis=0) / size
    return (
        jnp.concatenate(parts(forward), axis=0),
        jnp.concatenate(parts(inverse), axis=1),
    )


def matmul(left, right):
    return jnp.dot(left, right, preferred_element_type=F32)


def to_spectrum(rows, table):
    size = rows.shape[1]
    out = matmul(jnp.concatenate([rows, rows], axis=1), table)
    return out[:, :size], out[:, size:]


def from_spectrum(real, imag, table):
    size = real.shape[1]
    both = jnp.concatenate([real, imag], axis=1)
    high = both.astype(BF16)
    low = (both - high.astype(F32)).astype(BF16)
    out = matmul(high, table)
    return out[:, :size] + out[:, size:] + matmul(low, table[:, :size])


def split_rows(array, count):
    step = array.shape[0] // count
    return [array[i * step : (i + 1) * step] for i in range(count)]


def prepare_kernel(n, index_ref, *refs):
    given, (taps_ref, table_ref, inverse_ref) = refs[:n], refs[n : n + 3]
    grad_ref, filt_ref, tap_ref, filters, cotangents = refs[n + 3 :]
    s = index_ref[0]
    size = taps_ref.shape[1]
    for r in range(n):
        filters[s ^ r] = given[r][0]
        cotangents[s ^ r] = given[r][1]
    table = table_ref[...]
    filt_re, filt_im = to_spectrum(filters[...].reshape(n * size, size), table)
    cot_re, cot_im = to_spectrum(cotangents[...].reshape(n * size, size), table)
    filt_ref[:, :size] = filt_re
    filt_ref[:, size:] = filt_im
    taps = taps_ref[pl.ds(pl.multiple_of(s * size, size), size), :]
    taps_high = taps.astype(BF16)
    taps_low = (taps - taps_high.astype(F32)).astype(BF16)
    tap_re, tap_im = to_spectrum(taps_high, table)
    rest = matmul(taps_low, table[:size])
    tap_ref[:, :size] = tap_re + rest[:, :size]
    tap_ref[:, size:] = tap_im + rest[:, size:]
    fr, fi = split_rows(filt_re, n), split_rows(filt_im, n)
    cr, ci = split_rows(cot_re, n), split_rows(cot_im, n)
    turned = []
    for b in range(n):
        if b + 1 < n:
            turned.append((cr[b] + ci[b + 1], ci[b] - cr[b + 1]))
        else:
            turned.append((cr[b], ci[b]))
    real, imag = [], []
    for b in range(n):
        re, im = 0.0, 0.0
        for d in range(n - b):
            vr, vi = turned[b + d]
            re = re + fr[d] * vr + fi[d] * vi
            im = im + fr[d] * vi - fi[d] * vr
        real.append(re)
        imag.append(im)
    out = from_spectrum(jnp.concatenate(real), jnp.concatenate(imag), inverse_ref[...])
    grad_ref[...] = out.astype(BF16).reshape(n, size, size)


def gate_kernel(n, index_ref, *refs):
    blocks, refs = refs[:n], refs[n:]
    grad_in_ref, tap_ref, table_ref, inverse_ref = refs[:4]
    kept_ref, gated_ref, held, lent = refs[4], refs[5], refs[-1], refs[6:-1]
    c = index_ref[1]
    half, size = n // 2, tap_ref.shape[0]
    bits = n.bit_length() - 1
    for j in range(n):
        held[c ^ j ^ half] = blocks[j][...]
    values = held[...].reshape(n * size, size)
    table, inverse = table_ref[...], inverse_ref[...]
    tr, ti = tap_ref[:, :size], tap_ref[:, size:]
    wide = values.astype(F32)
    gate = jax.nn.sigmoid(wide)
    grad = grad_in_ref[...].reshape(n * size, size).astype(F32)
    grad_medium = (grad * gate).astype(BF16)
    re, im = to_spectrum(values, table)
    gr, gi = to_spectrum(grad_medium, table)
    re, im, gr, gi = (split_rows(x, n) for x in (re, im, gr, gi))
    real, imag, back_real, back_imag = [], [], [], []
    for b in range(n):
        ur, ui = (re[b] - im[b - 1], im[b] + re[b - 1]) if b else (re[b], im[b])
        real.append(tr * ur - ti * ui)
        imag.append(tr * ui + ti * ur)
        vr, vi = (gr[b] + gi[b + 1], gi[b] - gr[b + 1]) if b + 1 < n else (gr[b], gi[b])
        back_real.append(tr * vr + ti * vi)
        back_imag.append(tr * vi - ti * vr)
    medium = from_spectrum(jnp.concatenate(real), jnp.concatenate(imag), inverse)
    through = from_spectrum(jnp.concatenate(back_real), jnp.concatenate(back_imag), inverse)
    gated_ref[...] = (medium * gate).astype(BF16).reshape(n, size, size)
    back = (through + grad * medium * gate * (1.0 - gate)).astype(BF16)
    held[...] = back.reshape(n, size, size)
    for j in range(half):
        target = lent[j - 1] if j else kept_ref
        target[0] = held[reverse_bits(c ^ (half + j) ^ half, bits)]
        target[1] = held[reverse_bits(c ^ j ^ half, bits)]


def turned_side(s):
    return (s ^ (s >> 1)) & 1


def deal_kernel(n, index_ref, *refs):
    pairs, outs = refs[: n // 2], refs[n // 2 :]
    s = index_ref[0]
    for r in range(n):
        for j in range(n // 2):
            outs[r][j] = pairs[j][turned_side(s ^ r)]


def long_kernel(n, index_ref, *refs):
    pairs, (gated_ref, filt_ref, table_ref, inverse_ref) = refs[: n // 2], refs[n // 2 : n // 2 + 4]
    outs, held = refs[n // 2 + 4 : -1], refs[-1]
    s = index_ref[0]
    size = gated_ref.shape[2]
    re, im = to_spectrum(gated_ref[...].reshape(n * size, size), table_ref[...])
    re, im = split_rows(re, n), split_rows(im, n)
    fr, fi = split_rows(filt_ref[:, :size], n), split_rows(filt_ref[:, size:], n)
    turned = [(re[0], im[0])]
    for b in range(1, n):
        turned.append((re[b] - im[b - 1], im[b] + re[b - 1]))
    real, imag = [], []
    for b in range(n):
        zr, zi = 0.0, 0.0
        for d in range(b + 1):
            ur, ui = turned[b - d]
            zr = zr + fr[d] * ur - fi[d] * ui
            zi = zi + fr[d] * ui + fi[d] * ur
        real.append(zr)
        imag.append(zi)
    out = from_spectrum(jnp.concatenate(real), jnp.concatenate(imag), inverse_ref[...])
    held[...] = out.astype(BF16).reshape(n, size, size)
    for r in range(n):
        for j in range(n // 2):
            outs[r][j] = pairs[j][1 - turned_side(s ^ r)]
        outs[r][n // 2] = held[s ^ r]


def place_kernel(n, index_ref, *refs):
    given, out_ref = refs[:n], refs[n]
    s = index_ref[0]
    size = given[0].shape[1]
    for r in range(n):
        out_ref[pl.ds(pl.multiple_of((s ^ r) * size, size), size), :] = given[r][n // 2]


def arrange_kernel(n, index_ref, given_ref, filters_ref, cotangent_ref, *refs):
    weight_ref, turned_ref, blocks = refs[0], refs[1], refs[2:]
    s = index_ref[0]
    size = given_ref.shape[1] // n
    for r in range(n):
        start = pl.multiple_of((s ^ r) * size, size)
        blocks[r][0] = filters_ref[pl.ds(start, size), :]
        blocks[r][1] = cotangent_ref[pl.ds(start, size), :]
        block = given_ref[:, pl.ds(start, size)]
        weight_ref[:, r * size : (r + 1) * size] = block
        turned_ref[r * size : (r + 1) * size, :] = block.T


def values_kernel(n, *refs):
    half = n // 2
    weights, (upper_ref, lower_ref), outs = refs[:half], refs[half : half + 2], refs[half + 2 :]
    right = jnp.concatenate([upper_ref[...], lower_ref[...]], axis=0)
    step = weights[0].shape[0] // n
    for j in range(half):
        out = matmul(weights[j][...], right).astype(BF16)
        for r in range(n):
            outs[r][j] = out[r * step : (r + 1) * step]


def sum_kernel(n, *refs):
    terms, outs = refs[: -(n // 2)], refs[-(n // 2) :]
    for j, out_ref in enumerate(outs):
        total = terms[0][j].astype(F32)
        for term in terms[1:]:
            total = total + term[j].astype(F32)
        out_ref[...] = total.astype(BF16)


def input_kernel(n, *refs):
    half = n // 2
    weights, grads, outs = refs[:half], refs[half : half + n], refs[half + n :]
    total = 0.0
    for j in range(half):
        right = jnp.concatenate([ref[j] for ref in grads], axis=0)
        total = total + matmul(weights[j][...], right)
    rows = outs[0].shape[0]
    for k, out_ref in enumerate(outs):
        out_ref[...] = total[k * rows : (k + 1) * rows].astype(out_ref.dtype)


def total_kernel(k, near_ref, far_ref, out_ref):
    rows = far_ref.shape[0]
    near = near_ref[k * rows : (k + 1) * rows, :]
    out_ref[...] = (near + far_ref[...].astype(F32)).astype(BF16)


def cut_kernel(rows, given_ref, lower_ref, upper_ref, done):
    low = pltpu.make_async_copy(given_ref.at[rows:], lower_ref, done.at[0])
    high = pltpu.make_async_copy(given_ref.at[:rows], upper_ref, done.at[1])
    low.start()
    high.start()
    low.wait()
    high.wait()


def call(kernel, outs, scratch, index, args, flops, place=pltpu.VMEM):
    sizes = sum(math.prod(a.shape) * a.dtype.itemsize for a in (*args, *outs))
    held = sum(math.prod(a.shape) * 4 for a in scratch)
    specs = [pl.BlockSpec(memory_space=place)] * len(args)
    if index is not None:
        specs = [pl.BlockSpec(memory_space=pltpu.SMEM)] + specs
        args = (index, *args)
    return pl.pallas_call(
        kernel,
        out_shape=tuple(outs),
        in_specs=specs,
        out_specs=tuple(pl.BlockSpec(memory_space=pltpu.VMEM) for _ in outs),
        scratch_shapes=scratch,
        cost_estimate=pl.CostEstimate(flops=flops, bytes_accessed=sizes, transcendentals=0),
        compiler_params=pltpu.CompilerParams(vmem_limit_bytes=3 * (sizes + held) + (4 << 20)),
    )(*args)


def square_plan(n, activations, projection, medium_taps, long_filters, cotangent):
    bits = n.bit_length() - 1
    half = n // 2
    depth, size = activations.shape
    own = projection.shape[1] // n
    s, c = lax.axis_index("seq"), lax.axis_index("ch")
    index = jnp.stack([s, c]).astype(jnp.int32)
    shape = jax.ShapeDtypeStruct

    def move(array, target):
        pairs = [
            (i * n + j, (lambda t: t[0] * n + t[1])(target(i, j)))
            for i in range(n)
            for j in range(n)
        ]
        return lax.ppermute(array, ("seq", "ch"), pairs)

    def across_seq(array, step):
        return move(array, lambda i, j: (i ^ step, j))

    def across_ch(array, r):
        return move(array, lambda i, j: (i, j ^ r))

    def spread(parts):
        return [parts[0]] + [across_seq(parts[r], r) for r in range(1, n)]

    def lend(parts):
        return [parts[0]] + [across_ch(parts[j], j) for j in range(1, half)]

    low_rows = depth // 8
    lower, upper = call(
        functools.partial(cut_kernel, depth - low_rows),
        [shape((low_rows, size), BF16), shape((depth - low_rows, size), BF16)],
        [pltpu.SemaphoreType.DMA((2,))],
        None,
        (activations,),
        0,
        place=pl.ANY,
    )
    moved = across_ch(lower, half)
    upper = move(upper, lambda i, j: (j, i ^ half))
    lower = move(moved, lambda i, j: (j ^ half, i ^ half))
    weight, weight_t, *blocks = call(
        functools.partial(arrange_kernel, n),
        [shape(projection.shape, BF16), shape(projection.shape[::-1], BF16)]
        + [shape((2, own, size), BF16)] * n,
        [],
        index,
        (projection, long_filters, cotangent),
        0,
    )
    table, inverse = block_tables(size)
    weight, weight_t, table, inverse, *blocks = lax.optimization_barrier(
        (weight, weight_t, table, inverse, *blocks)
    )

    weights, weights_t = lend([weight] * half), lend([weight_t] * half)

    def values_of(upper, lower):
        parts = call(
            functools.partial(values_kernel, n),
            [shape((half, own, size), BF16)] * n,
            [],
            None,
            (*weights_t, upper, lower),
            2 * depth * n * own * half * size,
        )
        terms = spread(parts)
        sums = call(
            functools.partial(sum_kernel, n),
            [shape((own, size), BF16)] * half,
            [],
            None,
            tuple(terms),
            n * half * own * size,
        )
        return lend(sums)

    far_upper, far_lower = across_ch(upper, half), across_ch(lower, half)
    blocks = spread(blocks)
    near_values = values_of(upper, lower)
    far_values = values_of(far_upper, far_lower)

    spectrum = 4 * n * size * 2 * size * own
    grad_gated, filt, tap = call(
        functools.partial(prepare_kernel, n),
        [shape((n, own, size), BF16), shape((n * own, 2 * size), F32), shape((own, 2 * size), F32)],
        [pltpu.VMEM((n, own, size), BF16), pltpu.VMEM((n, own, size), BF16)],
        index,
        (*blocks, medium_taps, table, inverse),
        6 * spectrum,
    )
    kept, gated, *lent = call(
        functools.partial(gate_kernel, n),
        [shape((2, own, size), BF16), shape((n, own, size), BF16)]
        + [shape((2, own, size), BF16)] * (half - 1),
        [pltpu.VMEM((n, own, size), BF16)],
        index,
        (*near_values, *far_values, grad_gated, tap, table, inverse),
        8 * spectrum,
    )
    pairs = lend([kept, *lent])
    far_back = call(
        functools.partial(deal_kernel, n),
        [shape((half, own, size), BF16)] * n,
        [],
        index,
        tuple(pairs),
        0,
    )
    far_back = spread(far_back)

    near_back = call(
        functools.partial(long_kernel, n),
        [shape((half + 1, own, size), BF16)] * n,
        [pltpu.VMEM((n, own, size), BF16)],
        index,
        (*pairs, gated, filt, table, inverse),
        4 * spectrum,
    )
    near_back = spread(near_back)

    def input_of(parts, kind, pieces):
        return call(
            functools.partial(input_kernel, n),
            [shape((depth // pieces, size), kind)] * pieces,
            [],
            None,
            (*weights, *parts),
            2 * depth * n * own * half * size,
        )

    far_total = input_of(far_back, BF16, PIECES)
    (near_total,) = input_of(near_back, F32, 1)
    homes = []
    for k in range(PIECES):
        moved = across_ch(far_total[k], half)
        (total,) = call(
            functools.partial(total_kernel, k),
            [shape((depth // PIECES, size), BF16)],
            [],
            None,
            (near_total, moved),
            depth // PIECES * size,
        )
        homes.append(move(total, lambda i, j: (reverse_bits(j ^ half ^ half * turned_side(i), bits), i)))
    input_grad = jnp.concatenate(homes) if PIECES > 1 else homes[0]
    (conv_out,) = call(
        functools.partial(place_kernel, n),
        [shape((n * own, size), BF16)],
        [],
        index,
        tuple(near_back),
        0,
    )
    return conv_out, input_grad


def medium_forward(padded, tap_weights, length):
    tap_count = tap_weights.shape[1]
    summed = jnp.zeros((padded.shape[0], length), jnp.float32)
    for offset in range(tap_count):
        begin_col = tap_count - 1 - offset
        summed = (
            summed + tap_weights[:, offset : offset + 1] * padded[:, begin_col : begin_col + length]
        )
    return summed


def medium_backward(padded, tap_weights, length):
    tap_count = tap_weights.shape[1]
    summed = jnp.zeros((padded.shape[0], length), jnp.float32)
    for offset in range(tap_count):
        summed = summed + tap_weights[:, offset : offset + 1] * padded[:, offset : offset + length]
    return summed


def dft_tables(length):
    points = 2 * length
    columns = 128
    row_count = points // columns
    half_rows = row_count // 2
    freq_rows = jnp.arange(row_count, dtype=jnp.int32)
    time_rows = jnp.arange(half_rows, dtype=jnp.int32)
    lane_index = jnp.arange(columns, dtype=jnp.int32)
    angle_first = (
        2.0
        * math.pi
        / row_count
        * (freq_rows[:, None] * time_rows[None, :] % row_count).astype(jnp.float32)
    )
    angle_twist = (
        2.0
        * math.pi
        / points
        * (freq_rows[:, None] * lane_index[None, :] % points).astype(jnp.float32)
    )
    angle_last = (
        2.0
        * math.pi
        / columns
        * (lane_index[:, None] * lane_index[None, :] % columns).astype(jnp.float32)
    )
    return (
        jnp.cos(angle_first),
        jnp.sin(angle_first),
        jnp.cos(angle_twist),
        jnp.sin(angle_twist),
        jnp.cos(angle_last),
        jnp.sin(angle_last),
    )


def forward_dft(signal, tables):
    cos_first, sin_first, cos_twist, sin_twist, cos_last, sin_last = tables
    channels = signal.shape[0]
    shaped = signal.reshape(channels, cos_first.shape[1], 128)
    section_re = jnp.einsum("kn,cnq->ckq", cos_first, shaped, precision=exact_mode)
    section_im = -jnp.einsum("kn,cnq->ckq", sin_first, shaped, precision=exact_mode)
    twist_re = section_re * cos_twist + section_im * sin_twist
    twist_im = section_im * cos_twist - section_re * sin_twist
    spec_re = jnp.einsum("ckq,qm->ckm", twist_re, cos_last, precision=exact_mode) + jnp.einsum(
        "ckq,qm->ckm", twist_im, sin_last, precision=exact_mode
    )
    spec_im = jnp.einsum("ckq,qm->ckm", twist_im, cos_last, precision=exact_mode) - jnp.einsum(
        "ckq,qm->ckm", twist_re, sin_last, precision=exact_mode
    )
    return (spec_re, spec_im)


def inverse_dft(spec_re, spec_im, tables):
    cos_first, sin_first, cos_twist, sin_twist, cos_last, sin_last = tables
    channels = spec_re.shape[0]
    half_rows = cos_first.shape[1]
    inner_re = jnp.einsum("ckq,qm->ckm", spec_re, cos_last, precision=exact_mode) - jnp.einsum(
        "ckq,qm->ckm", spec_im, sin_last, precision=exact_mode
    )
    inner_im = jnp.einsum("ckq,qm->ckm", spec_im, cos_last, precision=exact_mode) + jnp.einsum(
        "ckq,qm->ckm", spec_re, sin_last, precision=exact_mode
    )
    turned_re = inner_re * cos_twist - inner_im * sin_twist
    turned_im = inner_im * cos_twist + inner_re * sin_twist
    output = jnp.einsum("kn,ckq->cnq", cos_first, turned_re, precision=exact_mode) - jnp.einsum(
        "kn,ckq->cnq", sin_first, turned_im, precision=exact_mode
    )
    points = 2 * half_rows * 128
    return (output / points).reshape(channels, half_rows * 128)


def causal_apply(signal, filt_re, filt_im, tables, conjugate):
    sig_re, sig_im = forward_dft(signal, tables)
    if conjugate:
        prod_re = sig_re * filt_re + sig_im * filt_im
        prod_im = sig_im * filt_re - sig_re * filt_im
    else:
        prod_re = sig_re * filt_re - sig_im * filt_im
        prod_im = sig_im * filt_re + sig_re * filt_im
    return inverse_dft(prod_re, prod_im, tables)


def on_device(activations, projection, medium_taps, long_filters, cotangent):
    tap_count = medium_taps.shape[1]
    whole_in = lax.all_gather(activations, "ch", axis=0, tiled=True)
    mixed_sum = lax.dot_general(
        lax.all_gather(projection, "seq", axis=0, tiled=True),
        whole_in,
        (((0,), (0,)), ((), ())),
        preferred_element_type=jnp.float32,
    )
    values = mixed_sum.astype(jnp.bfloat16)
    channel_count = values.shape[0] // lax.axis_size("seq")
    own_taps = lax.dynamic_slice_in_dim(
        medium_taps, lax.axis_index("seq") * channel_count, channel_count, 0
    )
    arrived, filters_ch = (
        lax.all_to_all(values, "seq", split_axis=0, concat_axis=1, tiled=True),
        lax.all_to_all(long_filters, "seq", split_axis=0, concat_axis=1, tiled=True),
    )
    tables = dft_tables(arrived.shape[1])
    filt_re, filt_im = forward_dft(filters_ch.astype(jnp.float32), tables)
    values_ch = arrived.astype(jnp.float32)
    padded_ch = jnp.pad(values_ch, ((0, 0), (tap_count - 1, 0)))
    conv_ch = medium_forward(padded_ch, own_taps, arrived.shape[1])
    gate_ch = jax.nn.sigmoid(values_ch)
    signal = lax.optimization_barrier((conv_ch * gate_ch).astype(jnp.bfloat16)).astype(jnp.float32)
    kept_state = (conv_ch, gate_ch)
    output_ch = causal_apply(signal, filt_re, filt_im, tables, False).astype(jnp.bfloat16)
    output_ch, context = (output_ch, (filt_re, filt_im, tables, kept_state))
    conv_out = lax.all_to_all(output_ch, "seq", split_axis=1, concat_axis=0, tiled=True)
    grad_ch = lax.all_to_all(cotangent, "seq", split_axis=0, concat_axis=1, tiled=True)
    filt_re, filt_im, tables, kept_state = context
    back_grad = lax.optimization_barrier(
        causal_apply(grad_ch.astype(jnp.float32), filt_re, filt_im, tables, True).astype(
            jnp.bfloat16
        )
    )
    conv_ch, gate_ch = kept_state
    grad_wide = back_grad.astype(jnp.float32)
    conv_grad = lax.optimization_barrier((grad_wide * gate_ch).astype(jnp.bfloat16)).astype(
        jnp.float32
    )
    padded_grad = jnp.pad(conv_grad, ((0, 0), (0, tap_count - 1)))
    through = medium_backward(padded_grad, own_taps, conv_grad.shape[1])
    gate_grad = grad_wide * conv_ch * gate_ch * (1.0 - gate_ch)
    back_ch = (through + gate_grad).astype(jnp.bfloat16)
    returned = lax.all_to_all(back_ch, "seq", split_axis=1, concat_axis=0, tiled=True)
    partial_grad = jnp.dot(
        lax.all_gather(projection, "seq", axis=0, tiled=True),
        returned,
        preferred_element_type=jnp.float32,
    )
    input_grad = lax.psum_scatter(
        partial_grad.astype(jnp.bfloat16), "ch", scatter_dimension=0, tiled=True
    )
    return (conv_out, input_grad)


def fits_square(mesh, activations, projection, medium_taps):
    seq, ch = mesh.shape["seq"], mesh.shape["ch"]
    size = activations.shape[1] // (mesh.shape["grp"] * seq)
    return (
        seq == ch
        and seq > 1
        and seq & (seq - 1) == 0
        and medium_taps.shape[1] == size
        and projection.shape[1] == seq * ch * size
        and size % 128 == 0
        and activations.shape[0] % (2 * ch * size) == 0
    )


def solution(mesh):
    n = mesh.shape["seq"]

    def placed(body):
        return jax.shard_map(
            body,
            mesh=mesh,
            in_specs=(
                P("ch", ("grp", "seq")),
                P("seq", "ch"),
                P("ch", None),
                P("ch", "seq"),
                P("ch", ("grp", "seq")),
            ),
            out_specs=(P("ch", ("grp", "seq")), P("ch", ("grp", "seq"))),
            check_vma=False,
        )

    def square(*args):
        return square_plan(n, *args)

    def step(*args):
        return placed(square if fits_square(mesh, *args[:3]) else on_device)(*args)

    if mesh.shape["seq"] != mesh.shape["ch"]:
        return step
    return step
```
